512 devices in a mesh: orb: 32 (over z, y_lo, core), dom: 16 (over x, y_hi).
Axes of the slice: x: 4, y: 8 (y_hi: 4, y_lo: 2; y = y_hi * 2 + y_lo), z: 8, core: 2. Of those that a mesh axis runs over, the one named last changes fastest.
Arguments:
- orbitals: bfloat16 [32, 16, 192, 128], P('orb', None, 'dom'), may hold values from -6 to 6
- potential: float32 [16, 192, 128], P(None, 'dom'), may hold values from 0 to 2
- degree: int32 [32], P('orb'), may hold values from 1 to 8, as said below
- owners: int32 [4], replicated, may hold values from 0 to 31
- rotation: bfloat16 [4, 1, 32], P(None, None, 'orb'), may hold values from -3 to 3
Outputs:
- filtered: float32 [32, 16, 192, 128], P('orb', None, 'dom')
- rotated: float32 [32, 16, 192, 128], P('orb', None, 'dom')
The draws below stay inside these ranges and needn't reach their ends.
Inputs may be any that keep to these rules, and one draw needn't show every extreme that they name: Every draw has an orbital of degree 8 and one of degree 1. `owners`: panel numbers; panel q holds orbital q alone.
All inputs are finite; a program needn't handle non-finite values.
Results may differ from the reference program's by a relative error of at most 0.0003.
Values sent between devices are 32-bit elements; how exact they have to be, the bound alone decides.
A program may use at most 64 MiB of HBM per device.

```python
import jax
import jax.numpy as jnp
from jax import lax

ORB_DEV = 1
PL = 16
GY = 128
RADIUS = 6
MAXDEG = 8
STEPS = 4
NORB = 32
PANEL = 1
NPANEL = 32
GX = 192
N_ORB = 32


def draw_degree(key, part):
    first_key, second_key, third_key = jax.random.split(key, 3)
    values = jax.random.randint(first_key, (NORB,), 1, MAXDEG + 1)
    top_place = jax.random.randint(second_key, (), 0, NORB)
    low_place = (top_place + 1 + jax.random.randint(third_key, (), 0, NORB - 1)) % NORB
    values = values.at[top_place].set(MAXDEG)
    values = values.at[low_place].set(1)
    return values.astype(jnp.int32)


def plant(drawn, rng, smallest, largest):
    dims = drawn.shape
    place = [jax.random.randint(jax.random.fold_in(rng, axis), (), 0, dims[axis]) for axis in range(len(dims))]
    drawn = drawn.at[tuple(place)].set(smallest)
    longest = dims.index(max(dims))
    place[longest] = (place[longest] + 1) % dims[longest]
    return drawn.at[tuple(place)].set(largest)


def steps_of(stream_key, shape, cuts, least, top_value):
    level = 1.0
    for dim, parts in cuts:
        steps = jax.random.uniform(jax.random.fold_in(jax.random.fold_in(stream_key, 6), dim), (parts,), jnp.float32, least / len(cuts), top_value / len(cuts))
        level = level * jnp.repeat(jnp.exp(steps), shape[dim] // parts).reshape((-1,) + (1,) * (len(shape) - 1 - dim))
    return level


def bell_draw(key, extent, spread, most, pieces=(), kind=jnp.bfloat16):
    factor_of = steps_of(key, extent, pieces, -0.22, 0.18) if pieces else 1.0
    entries = jax.random.normal(key, extent, jnp.float32) * spread * factor_of
    return jnp.minimum(jnp.maximum(entries, -most), most).astype(kind)


def setup_inputs(seed: int = 0) -> dict:
    key_of = jax.random.split(jax.random.key(seed), 6)
    orbitals = bell_draw(key_of[0], (NORB, PL, GX, GY), 1.0, 6.0, ((0, 32), (2, 16)))
    potential = jnp.clip(2.0 * jax.random.uniform(key_of[1], (PL, GX, GY), jnp.float32) ** steps_of(key_of[1], (PL, GX, GY), ((1, 16),), -0.2, 0.2), 0.0, 2.0)
    degree = draw_degree(jax.random.fold_in(key_of[5], 71), 0)
    owners = plant(jax.random.randint(key_of[3], (STEPS,), 0, NPANEL), jax.random.fold_in(key_of[3], 1), 0, NPANEL - 1).astype(jnp.int32)
    rotation = bell_draw(key_of[4], (STEPS, PANEL, NORB), (STEPS * PANEL) ** -0.5, 3.0, ((2, 32),))
    return dict(orbitals=orbitals, potential=potential, degree=degree, owners=owners, rotation=rotation)


STENCIL = (-5369.0 / 1800.0, 12.0 / 7.0, -15.0 / 56.0, 10.0 / 189.0, -1.0 / 112.0, 2.0 / 1925.0, -1.0 / 16632.0)
FILTER_CENTER = 7.75
FILTER_HALF = 6.25


def apply_hamiltonian(padded, potential):
    width = padded.shape[2] - 2 * RADIUS
    center = padded[:, :, RADIUS:RADIUS + width]
    laplace = (3.0 * STENCIL[0]) * center
    for offset in range(1, RADIUS + 1):
        beside = padded[:, :, RADIUS + offset:RADIUS + offset + width] + padded[:, :, RADIUS - offset:RADIUS - offset + width]
        beside = beside + jnp.roll(center, offset, 3) + jnp.roll(center, -offset, 3)
        beside = beside + jnp.roll(center, offset, 1) + jnp.roll(center, -offset, 1)
        laplace = laplace + STENCIL[offset] * beside
    return -0.5 * laplace + potential * center


def chebyshev_next(applied, current, previous, first):
    shifted = applied - FILTER_CENTER * current
    if first:
        return shifted / FILTER_HALF
    return (2.0 / FILTER_HALF) * shifted - previous


def reference(orbitals, potential, degree, owners, rotation):
    blocks = orbitals.reshape(N_ORB, ORB_DEV, PL, GX, GY)
    degrees = degree.reshape(N_ORB, ORB_DEV)

    def one_block(pair):
        block, degree_block = pair
        current = block.astype(jnp.float32)
        previous = current
        selected = jnp.zeros_like(current)
        for section in range(MAXDEG):
            padded = jnp.pad(current, ((0, 0), (0, 0), (RADIUS, RADIUS), (0, 0)))
            applied = apply_hamiltonian(padded, potential)
            advanced = chebyshev_next(applied, current, previous, section == 0)
            selected = jnp.where((degree_block == section + 1)[:, None, None, None], advanced, selected)
            previous, current = current, advanced
        return selected

    filtered = lax.map(one_block, (blocks, degrees)).reshape(NORB, PL, GX, GY)
    flattened = filtered.reshape(NORB, PL * GX * GY)
    rotated = jnp.zeros((NORB, PL * GX * GY), jnp.float32)
    for section in range(STEPS):
        start_row = (owners[section] * PANEL).astype(jnp.int32)
        panel = lax.dynamic_slice_in_dim(flattened, start_row, PANEL, 0)
        coefficients = rotation[section].astype(jnp.float32)
        rotated = rotated + lax.dot_general(coefficients, panel, (((0,), (0,)), ((), ())), precision=lax.Precision.HIGHEST, preferred_element_type=jnp.float32)
    rotated = rotated.reshape(NORB, PL, GX, GY)
    return filtered, rotated
```

```python
import jax
import jax.numpy as jnp
import numpy as np
from jax import lax
from jax.experimental import pallas as pl
from jax.experimental.pallas import tpu as pltpu
from jax.sharding import PartitionSpec as P

RADIUS = 6
MAXDEG = 8
STEPS = 4
ROUNDS = 4
STENCIL = (
    -5369.0 / 1800.0,
    12.0 / 7.0,
    -15.0 / 56.0,
    10.0 / 189.0,
    -1.0 / 112.0,
    2.0 / 1925.0,
    -1.0 / 16632.0,
)
FILTER_CENTER = 7.75
FILTER_HALF = 6.25
SCALE = 2.0 / FILTER_HALF
MESH = pl.DeviceIdType.MESH

SIDE = [-0.5 * SCALE * c for c in STENCIL]
CENTRE = 3.0 * SIDE[0] - SCALE * FILTER_CENTER


def circulant(size):
    matrix = np.zeros((size, size), np.float64)
    for offset in range(1, RADIUS + 1):
        for index in range(size):
            matrix[index, (index + offset) % size] += SIDE[offset]
            matrix[index, (index - offset) % size] += SIDE[offset]
    return matrix


def halves(matrix):
    high = matrix.astype(jnp.bfloat16)
    low = (matrix - high.astype(np.float64)).astype(jnp.bfloat16)
    return high, low


def stencil_matrices(planes, cells, layers):
    high, low = halves(circulant(cells))
    along_y = np.block([[high, low], [high, low]])
    high, low = halves(np.kron(np.eye(layers), circulant(planes)))
    along_p = np.block([[high, high], [low, low]])
    return along_y, along_p


def filter_kernel(width, orb_ref, pot_ref, degree_ref, ymat_ref, pmat_ref, out_ref,
                  field, inner, diag, send_sem, recv_sem, pot_send, pot_recv):
    count = lax.axis_size("dom")
    me = lax.axis_index("dom")
    has_left = me > 0
    has_right = me < count - 1
    half = RADIUS
    w = width

    def to_left(src, dst, ssem, rsem):
        return pltpu.make_async_remote_copy(
            src_ref=src, dst_ref=dst, send_sem=ssem, recv_sem=rsem,
            device_id={"dom": jnp.maximum(me - 1, 0)}, device_id_type=MESH)

    def to_right(src, dst, ssem, rsem):
        return pltpu.make_async_remote_copy(
            src_ref=src, dst_ref=dst, send_sem=ssem, recv_sem=rsem,
            device_id={"dom": jnp.minimum(me + 1, count - 1)}, device_id_type=MESH)

    def copies(r):
        src = orb_ref if r == 0 else field.at[r, pl.ds(w, w)]
        left = to_left(src, field.at[r, pl.ds(2 * w, w)], send_sem.at[r, 0], recv_sem.at[r, 0])
        right = to_right(src, field.at[r, pl.ds(0, w)], send_sem.at[r, 1], recv_sem.at[r, 1])
        return left, right

    pot_left = to_left(pot_ref.at[pl.ds(0, half)], diag.at[pl.ds(half + w, half)], pot_send.at[0], pot_recv.at[0])
    pot_right = to_right(pot_ref.at[pl.ds(w - half, half)], diag.at[pl.ds(0, half)], pot_send.at[1], pot_recv.at[1])

    barrier = pltpu.get_barrier_semaphore()

    for shift in (1, count - 1):
        pl.semaphore_signal(
            barrier, inc=1, device_id={"dom": lax.rem(me + shift, count)}, device_id_type=MESH)
    pl.semaphore_wait(barrier, 2)

    def start(r):
        left, right = copies(r)

        @pl.when(has_left)
        def _():
            left.start()
            if r == 0:
                pot_left.start()

        @pl.when(has_right)
        def _():
            right.start()
            if r == 0:
                pot_right.start()

    def arrive(r):
        left, right = copies(r)

        @pl.when(has_left)
        def _():
            right.wait_recv()
            if r == 0:
                pot_right.wait_recv()

        @pl.when(has_right)
        def _():
            left.wait_recv()
            if r == 0:
                pot_left.wait_recv()

    start(0)

    @pl.when(jnp.logical_not(has_left))
    def _():
        for r in range(ROUNDS):
            field[r, 0:w] = jnp.zeros((w,) + field.shape[2:], jnp.float32)
        diag[0:half] = jnp.zeros((half,) + diag.shape[1:], jnp.float32)

    @pl.when(jnp.logical_not(has_right))
    def _():
        for r in range(ROUNDS):
            field[r, 2 * w:3 * w] = jnp.zeros((w,) + field.shape[2:], jnp.float32)
        diag[half + w:2 * half + w] = jnp.zeros((half,) + diag.shape[1:], jnp.float32)

    field[0, w:2 * w] = orb_ref[...]
    diag[half:half + w] = pot_ref[...]

    planes, cells = field.shape[2], field.shape[3]
    rows = half * planes
    left_mask = jnp.where(has_left, 1.0, 0.0).astype(jnp.float32)
    right_mask = jnp.where(has_right, 1.0, 0.0).astype(jnp.float32)
    degree = degree_ref[0]

    def applied(ref, low, diag_low):
        centre = ref[pl.ds(low, w)]
        total = (diag[pl.ds(diag_low, w)] * SCALE + CENTRE) * centre
        for offset in range(1, RADIUS + 1):
            total = total + SIDE[offset] * (ref[pl.ds(low + offset, w)] + ref[pl.ds(low - offset, w)])
        flat = centre.reshape(2 * rows, cells)
        high = flat.astype(jnp.bfloat16)
        rest = (flat - high.astype(jnp.float32)).astype(jnp.bfloat16)
        both = jnp.dot(jnp.concatenate([high, rest], axis=1), ymat_ref[...], preferred_element_type=jnp.float32)
        total = total + (both[:, :cells] + both[:, cells:]).reshape(centre.shape)
        stacked = jnp.concatenate([
            jnp.concatenate([high[:rows], high[rows:]], axis=1),
            jnp.concatenate([rest[:rows], rest[rows:]], axis=1)], axis=0)
        both = jnp.dot(pmat_ref[...], stacked, preferred_element_type=jnp.float32)
        both = both[:rows] + both[rows:]
        both = jnp.concatenate([both[:, :cells], both[:, cells:]], axis=0)
        return total + both.reshape(centre.shape)

    for r in range(ROUNDS):
        arrive(r)
        now = field.at[r]
        for part in range(2):
            low = part * w
            advanced = applied(now, low + half, low)
            if r == 0:
                advanced = 0.5 * advanced
            else:
                advanced = advanced - inner[low:low + w]
            if part == 0:
                inner[0:half] = advanced[:half] * left_mask
                inner[half:w] = advanced[half:]
            else:
                inner[w:w + half] = advanced[:half]
                inner[w + half:2 * w] = advanced[half:] * right_mask
        advanced = applied(inner, half, half) - now[w:2 * w]
        if r + 1 < ROUNDS:
            field[r + 1, w:2 * w] = advanced
            start(r + 1)
        before = out_ref[...] if r > 0 else jnp.zeros_like(advanced)
        before = jnp.where(degree == 2 * r + 1, inner[half:half + w], before)
        out_ref[...] = jnp.where(degree == 2 * r + 2, advanced, before)

    @pl.when(has_left)
    def _():
        for r in range(ROUNDS):
            copies(r)[0].wait_send()
        pot_left.wait_send()

    @pl.when(has_right)
    def _():
        for r in range(ROUNDS):
            copies(r)[1].wait_send()
        pot_right.wait_send()


def filtered_layers(orbitals, potential, degree):
    width, planes, cells = orbitals.shape
    ymat, pmat = stencil_matrices(planes, cells, RADIUS)
    vmem = pl.BlockSpec(memory_space=pltpu.VMEM)
    smem = pl.BlockSpec(memory_space=pltpu.SMEM)
    return pl.pallas_call(
        lambda *refs: filter_kernel(width, *refs),
        out_shape=jax.ShapeDtypeStruct(orbitals.shape, jnp.float32),
        in_specs=[vmem, vmem, smem, vmem, vmem],
        out_specs=vmem,
        scratch_shapes=[
            pltpu.VMEM((ROUNDS, 3 * width, planes, cells), jnp.float32),
            pltpu.VMEM((2 * width, planes, cells), jnp.float32),
            pltpu.VMEM((width + 2 * RADIUS, planes, cells), jnp.float32),
            pltpu.SemaphoreType.DMA((ROUNDS, 2)),
            pltpu.SemaphoreType.DMA((ROUNDS, 2)),
            pltpu.SemaphoreType.DMA((2,)),
            pltpu.SemaphoreType.DMA((2,)),
        ],
        compiler_params=pltpu.CompilerParams(collective_id=0, has_side_effects=True),
        name="chebyshev",
    )(orbitals, potential, degree, jnp.asarray(ymat), jnp.asarray(pmat))


def from_root(shard, axis, root):
    mine = lax.axis_index(axis) == root
    return lax.psum(jnp.where(mine, shard, jnp.zeros_like(shard)), axis)


def per_device(orbitals, potential, degree, owners, rotation):
    layers = jnp.transpose(orbitals[0].astype(jnp.float32), (1, 0, 2))
    selected = filtered_layers(layers, jnp.transpose(potential, (1, 0, 2)), degree)
    selected = jnp.transpose(selected, (1, 0, 2))[None]
    rotated = jnp.zeros(selected.shape, jnp.float32)
    for section in range(STEPS):
        panel = from_root(selected, "orb", owners[section])
        rotated = rotated + rotation[section, 0, 0].astype(jnp.float32) * panel
    return (selected, rotated)


def solution(mesh):
    placed = (
        P("orb", None, "dom", None),
        P(None, "dom", None),
        P("orb"),
        P(),
        P(None, None, "orb"),
    )
    return jax.shard_map(
        per_device,
        mesh=mesh,
        in_specs=placed,
        out_specs=(P("orb", None, "dom", None), P("orb", None, "dom", None)),
        check_vma=False,
    )
```

```python
import jax
import jax.numpy as jnp
import numpy as np
from jax import lax
from jax.experimental import pallas as pl
from jax.experimental.pallas import tpu as pltpu
from jax.sharding import PartitionSpec as P

RADIUS = 6
MAXDEG = 8
STEPS = 4
ROUNDS = 4
STENCIL = (
    -5369.0 / 1800.0,
    12.0 / 7.0,
    -15.0 / 56.0,
    10.0 / 189.0,
    -1.0 / 112.0,
    2.0 / 1925.0,
    -1.0 / 16632.0,
)
FILTER_CENTER = 7.75
FILTER_HALF = 6.25
SCALE = 2.0 / FILTER_HALF
MESH = pl.DeviceIdType.MESH

SIDE = [-0.5 * SCALE * c for c in STENCIL]
CENTRE = 3.0 * SIDE[0] - SCALE * FILTER_CENTER


def circulant(size):
    matrix = np.zeros((size, size), np.float64)
    for offset in range(1, RADIUS + 1):
        for index in range(size):
            matrix[index, (index + offset) % size] += SIDE[offset]
            matrix[index, (index - offset) % size] += SIDE[offset]
    return matrix


def halves(matrix):
    high = matrix.astype(jnp.bfloat16)
    low = (matrix - high.astype(np.float64)).astype(jnp.bfloat16)
    return high, low


def stencil_matrices(planes, cells, layers):
    high, low = halves(circulant(cells))
    along_y = np.block([[high, low], [high, low]])
    high, low = halves(np.kron(np.eye(layers), circulant(planes)))
    along_p = np.block([[high, high], [low, low]])
    return along_y, along_p


def seat():
    orb = lax.axis_index("orb")
    return orb // 4, lax.rem(orb // 2, 2), lax.rem(orb, 2)


def at(z, pair, core):
    return {"orb": z * 4 + pair * 2 + core}


def by_distance(chips):
    return sorted(range(1, chips), key=lambda step: (min(step, chips - step), step))


def rotation_peers():
    chips = lax.axis_size("orb") // 4
    z, pair, core = seat()
    return [at(z, pair, 1 - core), at(z, 1 - pair, core)] + [
        at(lax.rem(z + step, chips), pair, core) for step in by_distance(chips)]


def rotate(filtered, owner_ref, rot_ref, rotated_ref, own, give, got_core, give_pair, got_pair,
           give_z, got_z, panels, sems):
    chips = lax.axis_size("orb") // 4
    z, pair, core = seat()
    orb = lax.axis_index("orb")
    near = by_distance(chips)
    chunk_of = lambda step: lax.rem(z + step, chips)
    mate, across = at(z, pair, 1 - core), at(z, 1 - pair, core)

    def copy(stage, src, dst, slot, peer, landing=None):
        return pltpu.make_async_remote_copy(
            src_ref=src, dst_ref=dst, send_sem=sems.at[stage, 0, slot],
            recv_sem=sems.at[stage, 1, slot if landing is None else landing],
            device_id=peer, device_id_type=MESH)

    def to_mate(k):
        return copy(0, give.at[:, k], got_core.at[:, k], k, mate)

    def to_across(k):
        return copy(1, give_pair.at[k], got_pair.at[k], k, across)

    def scatter(k):
        return copy(2, give_z.at[k], got_z.at[z], k, at(k, pair, core), z)

    def scattered(k):
        return copy(2, give_z.at[k], got_z.at[k], k, at(k, pair, core))

    def gather(k):
        piece = panels.at[core, pair, z]
        return copy(3, piece, piece, k, at(k, pair, core), z)

    def gathered(k):
        piece = panels.at[core, pair, k]
        return copy(3, piece, piece, k, at(k, pair, core))

    def share_across(k):
        piece = panels.at[core, pair, k]
        return copy(4, piece, piece, k, across)

    def shared_across(k):
        piece = panels.at[core, 1 - pair, k]
        return copy(4, piece, piece, k, across)

    def share_mate(k, which):
        piece = panels.at[core, which, k]
        return copy(5, piece, piece, which * chips + k, mate)

    def shared_mate(k, which):
        piece = panels.at[1 - core, which, k]
        return copy(5, piece, piece, which * chips + k, mate)

    own[...] = filtered.reshape(own.shape)

    def masked(panel, k):
        return jnp.where(owner_ref[panel] == orb, own[k], 0.0)

    far_first = near[::-1] + [0]
    for step in far_first:
        k = chunk_of(step)
        for which in range(2):
            give[which, k] = masked(2 * which + 1 - core, k)
        to_mate(k).start()
    for step in far_first:
        k = chunk_of(step)
        to_mate(k).wait_recv()
        give_pair[k] = got_core[1 - pair, k] + masked(2 * (1 - pair) + core, k)
        to_across(k).start()
    for step in far_first:
        k = chunk_of(step)
        to_across(k).wait_recv()
        part = got_core[pair, k] + masked(2 * pair + core, k) + got_pair[k]
        if step == 0:
            got_z[z] = part
        else:
            give_z[k] = part
            scatter(k).start()
    for step in near:
        scattered(chunk_of(step)).wait_recv()
    total = got_z[0]
    for k in range(1, chips):
        total = total + got_z[k]
    panels[core, pair, z] = total
    for step in near[::-1]:
        gather(chunk_of(step)).start()
    for step in [0] + near:
        k = chunk_of(step)
        if step != 0:
            gathered(k).wait_recv()
        share_across(k).start()
        share_mate(k, pair).start()
    for step in [0] + near:
        k = chunk_of(step)
        shared_across(k).wait_recv()
        share_mate(k, 1 - pair).start()
    for step in [0] + near:
        k = chunk_of(step)
        shared_mate(k, pair).wait_recv()
        shared_mate(k, 1 - pair).wait_recv()
        rotated_ref[k] = (rot_ref[0] * panels[0, 0, k] + rot_ref[1] * panels[1, 0, k]
                          + rot_ref[2] * panels[0, 1, k] + rot_ref[3] * panels[1, 1, k])
    for step in [0] + near:
        k = chunk_of(step)
        to_mate(k).wait_send()
        to_across(k).wait_send()
        if step != 0:
            scatter(k).wait_send()
            gather(k).wait_send()
        share_across(k).wait_send()
        share_mate(k, pair).wait_send()
        share_mate(k, 1 - pair).wait_send()


def filter_kernel(width, orb_ref, pot_ref, degree_ref, owner_ref, rot_ref, ymat_ref, pmat_ref,
                  out_ref, rotated_ref, field, inner, diag, send_sem, recv_sem, pot_send, pot_recv,
                  *rotation_scratch):
    count = lax.axis_size("dom")
    me = lax.axis_index("dom")
    has_left = me > 0
    has_right = me < count - 1
    half = RADIUS
    w = width

    def to_left(src, dst, ssem, rsem):
        return pltpu.make_async_remote_copy(
            src_ref=src, dst_ref=dst, send_sem=ssem, recv_sem=rsem,
            device_id={"dom": jnp.maximum(me - 1, 0)}, device_id_type=MESH)

    def to_right(src, dst, ssem, rsem):
        return pltpu.make_async_remote_copy(
            src_ref=src, dst_ref=dst, send_sem=ssem, recv_sem=rsem,
            device_id={"dom": jnp.minimum(me + 1, count - 1)}, device_id_type=MESH)

    def copies(r):
        src = orb_ref if r == 0 else field.at[r, pl.ds(w, w)]
        left = to_left(src, field.at[r, pl.ds(2 * w, w)], send_sem.at[r, 0], recv_sem.at[r, 0])
        right = to_right(src, field.at[r, pl.ds(0, w)], send_sem.at[r, 1], recv_sem.at[r, 1])
        return left, right

    pot_left = to_left(pot_ref.at[pl.ds(0, half)], diag.at[pl.ds(half + w, half)], pot_send.at[0], pot_recv.at[0])
    pot_right = to_right(pot_ref.at[pl.ds(w - half, half)], diag.at[pl.ds(0, half)], pot_send.at[1], pot_recv.at[1])

    barrier = pltpu.get_barrier_semaphore()

    peers = [{"dom": lax.rem(me + shift, count)} for shift in (1, count - 1)] + rotation_peers()
    for peer in peers:
        pl.semaphore_signal(barrier, inc=1, device_id=peer, device_id_type=MESH)
    pl.semaphore_wait(barrier, len(peers))

    def start(r):
        left, right = copies(r)

        @pl.when(has_left)
        def _():
            left.start()
            if r == 0:
                pot_left.start()

        @pl.when(has_right)
        def _():
            right.start()
            if r == 0:
                pot_right.start()

    def arrive(r):
        left, right = copies(r)

        @pl.when(has_left)
        def _():
            right.wait_recv()
            if r == 0:
                pot_right.wait_recv()

        @pl.when(has_right)
        def _():
            left.wait_recv()
            if r == 0:
                pot_left.wait_recv()

    start(0)

    @pl.when(jnp.logical_not(has_left))
    def _():
        for r in range(ROUNDS):
            field[r, 0:w] = jnp.zeros((w,) + field.shape[2:], jnp.float32)
        diag[0:half] = jnp.zeros((half,) + diag.shape[1:], jnp.float32)

    @pl.when(jnp.logical_not(has_right))
    def _():
        for r in range(ROUNDS):
            field[r, 2 * w:3 * w] = jnp.zeros((w,) + field.shape[2:], jnp.float32)
        diag[half + w:2 * half + w] = jnp.zeros((half,) + diag.shape[1:], jnp.float32)

    field[0, w:2 * w] = orb_ref[...]
    diag[half:half + w] = pot_ref[...]

    planes, cells = field.shape[2], field.shape[3]
    rows = half * planes
    left_mask = jnp.where(has_left, 1.0, 0.0).astype(jnp.float32)
    right_mask = jnp.where(has_right, 1.0, 0.0).astype(jnp.float32)
    degree = degree_ref[0]

    def applied(ref, low, diag_low):
        centre = ref[pl.ds(low, w)]
        total = (diag[pl.ds(diag_low, w)] * SCALE + CENTRE) * centre
        for offset in range(1, RADIUS + 1):
            total = total + SIDE[offset] * (ref[pl.ds(low + offset, w)] + ref[pl.ds(low - offset, w)])
        flat = centre.reshape(2 * rows, cells)
        high = flat.astype(jnp.bfloat16)
        rest = (flat - high.astype(jnp.float32)).astype(jnp.bfloat16)
        both = jnp.dot(jnp.concatenate([high, rest], axis=1), ymat_ref[...], preferred_element_type=jnp.float32)
        total = total + (both[:, :cells] + both[:, cells:]).reshape(centre.shape)
        stacked = jnp.concatenate([
            jnp.concatenate([high[:rows], high[rows:]], axis=1),
            jnp.concatenate([rest[:rows], rest[rows:]], axis=1)], axis=0)
        both = jnp.dot(pmat_ref[...], stacked, preferred_element_type=jnp.float32)
        both = both[:rows] + both[rows:]
        both = jnp.concatenate([both[:, :cells], both[:, cells:]], axis=0)
        return total + both.reshape(centre.shape)

    for r in range(ROUNDS):
        arrive(r)
        now = field.at[r]
        for part in range(2):
            low = part * w
            advanced = applied(now, low + half, low)
            if r == 0:
                advanced = 0.5 * advanced
            else:
                advanced = advanced - inner[low:low + w]
            if part == 0:
                inner[0:half] = advanced[:half] * left_mask
                inner[half:w] = advanced[half:]
            else:
                inner[w:w + half] = advanced[:half]
                inner[w + half:2 * w] = advanced[half:] * right_mask
        advanced = applied(inner, half, half) - now[w:2 * w]
        if r + 1 < ROUNDS:
            field[r + 1, w:2 * w] = advanced
            start(r + 1)
        before = out_ref[...] if r > 0 else jnp.zeros_like(advanced)
        before = jnp.where(degree == 2 * r + 1, inner[half:half + w], before)
        out_ref[...] = jnp.where(degree == 2 * r + 2, advanced, before)

    rotate(out_ref[...], owner_ref, rot_ref, rotated_ref, *rotation_scratch)

    @pl.when(has_left)
    def _():
        for r in range(ROUNDS):
            copies(r)[0].wait_send()
        pot_left.wait_send()

    @pl.when(has_right)
    def _():
        for r in range(ROUNDS):
            copies(r)[1].wait_send()
        pot_right.wait_send()


def filter_and_rotate(orbitals, potential, degree, owners, coefficients):
    width, planes, cells = orbitals.shape
    chips = lax.axis_size("orb") // 4
    piece = (width * planes // 8 // chips, 8, cells)
    ymat, pmat = stencil_matrices(planes, cells, RADIUS)
    vmem = pl.BlockSpec(memory_space=pltpu.VMEM)
    smem = pl.BlockSpec(memory_space=pltpu.SMEM)
    buffer = lambda *lead: pltpu.VMEM(lead + piece, jnp.float32)
    filtered, rotated = pl.pallas_call(
        lambda *refs: filter_kernel(width, *refs),
        out_shape=(
            jax.ShapeDtypeStruct(orbitals.shape, jnp.float32),
            jax.ShapeDtypeStruct((chips,) + piece, jnp.float32),
        ),
        in_specs=[vmem, vmem, smem, smem, smem, vmem, vmem],
        out_specs=(vmem, vmem),
        scratch_shapes=[
            pltpu.VMEM((ROUNDS, 3 * width, planes, cells), jnp.float32),
            pltpu.VMEM((2 * width, planes, cells), jnp.float32),
            pltpu.VMEM((width + 2 * RADIUS, planes, cells), jnp.float32),
            pltpu.SemaphoreType.DMA((ROUNDS, 2)),
            pltpu.SemaphoreType.DMA((ROUNDS, 2)),
            pltpu.SemaphoreType.DMA((2,)),
            pltpu.SemaphoreType.DMA((2,)),
            buffer(chips), buffer(2, chips), buffer(2, chips), buffer(chips), buffer(chips),
            buffer(chips), buffer(chips), buffer(2, 2, chips),
            pltpu.SemaphoreType.DMA((6, 2, 2 * chips)),
        ],
        compiler_params=pltpu.CompilerParams(collective_id=0, has_side_effects=True),
        name="filter_rotate",
    )(orbitals, potential, degree, owners, coefficients, jnp.asarray(ymat), jnp.asarray(pmat))
    return filtered, rotated.reshape(orbitals.shape)


def per_device(orbitals, potential, degree, owners, rotation):
    layers = jnp.transpose(orbitals[0].astype(jnp.float32), (1, 0, 2))
    filtered, rotated = filter_and_rotate(
        layers, jnp.transpose(potential, (1, 0, 2)), degree, owners,
        rotation.astype(jnp.float32).reshape(STEPS))
    return jnp.transpose(filtered, (1, 0, 2))[None], jnp.transpose(rotated, (1, 0, 2))[None]


def solution(mesh):
    placed = (
        P("orb", None, "dom", None),
        P(None, "dom", None),
        P("orb"),
        P(),
        P(None, None, "orb"),
    )
    return jax.shard_map(
        per_device,
        mesh=mesh,
        in_specs=placed,
        out_specs=(P("orb", None, "dom", None), P("orb", None, "dom", None)),
        check_vma=False,
    )
```

```python
import jax
import jax.numpy as jnp
import numpy as np
from jax import lax
from jax.experimental import pallas as pl
from jax.experimental.pallas import tpu as pltpu
from jax.sharding import PartitionSpec as P

RADIUS = 6
MAXDEG = 8
STEPS = 4
ROUNDS = 4
STENCIL = (
    -5369.0 / 1800.0,
    12.0 / 7.0,
    -15.0 / 56.0,
    10.0 / 189.0,
    -1.0 / 112.0,
    2.0 / 1925.0,
    -1.0 / 16632.0,
)
FILTER_CENTER = 7.75
FILTER_HALF = 6.25
SCALE = 2.0 / FILTER_HALF
MESH = pl.DeviceIdType.MESH

SIDE = [-0.5 * SCALE * c for c in STENCIL]
CENTRE = 3.0 * SIDE[0] - SCALE * FILTER_CENTER


def circulant(size):
    matrix = np.zeros((size, size), np.float64)
    for offset in range(1, RADIUS + 1):
        for index in range(size):
            matrix[index, (index + offset) % size] += SIDE[offset]
            matrix[index, (index - offset) % size] += SIDE[offset]
    return matrix


def halves(matrix):
    high = matrix.astype(jnp.bfloat16)
    low = (matrix - high.astype(np.float64)).astype(jnp.bfloat16)
    return high, low


def stencil_matrices(planes, cells, layers):
    high, low = halves(circulant(cells))
    along_y = np.block([[high, low], [high, low]])
    high, low = halves(np.kron(np.eye(layers), circulant(planes)))
    along_p = np.block([[high, high], [low, low]])
    return along_y, along_p


def seat():
    orb = lax.axis_index("orb")
    return orb // 4, lax.rem(orb // 2, 2), lax.rem(orb, 2)


def at(z, pair, core):
    return {"orb": z * 4 + pair * 2 + core}


def by_distance(chips):
    return sorted(range(1, chips), key=lambda step: (min(step, chips - step), step))


def rotation_peers():
    chips = lax.axis_size("orb") // 4
    z, pair, core = seat()
    return [at(z, pair, 1 - core), at(z, 1 - pair, core)] + [
        at(lax.rem(z + step, chips), pair, core) for step in by_distance(chips)]


def rotate(filtered, owner_ref, rot_ref, rotated_ref, own, give, got_core, give_pair, got_pair,
           give_z, got_z, panels, sems):
    chips = lax.axis_size("orb") // 4
    z, pair, core = seat()
    orb = lax.axis_index("orb")
    near = by_distance(chips)
    chunk_of = lambda step: lax.rem(z + step, chips)
    mate, across = at(z, pair, 1 - core), at(z, 1 - pair, core)

    def copy(stage, src, dst, slot, peer, landing=None):
        return pltpu.make_async_remote_copy(
            src_ref=src, dst_ref=dst, send_sem=sems.at[stage, 0, slot],
            recv_sem=sems.at[stage, 1, slot if landing is None else landing],
            device_id=peer, device_id_type=MESH)

    def to_mate(k):
        return copy(0, give.at[:, k], got_core.at[:, k], k, mate)

    def to_across(k):
        return copy(1, give_pair.at[k], got_pair.at[k], k, across)

    def scatter(k):
        return copy(2, give_z.at[k], got_z.at[z], k, at(k, pair, core), z)

    def scattered(k):
        return copy(2, give_z.at[k], got_z.at[k], k, at(k, pair, core))

    def gather(k):
        piece = panels.at[core, pair, z]
        return copy(3, piece, piece, k, at(k, pair, core), z)

    def gathered(k):
        piece = panels.at[core, pair, k]
        return copy(3, piece, piece, k, at(k, pair, core))

    def share_across(k):
        piece = panels.at[core, pair, k]
        return copy(4, piece, piece, k, across)

    def shared_across(k):
        piece = panels.at[core, 1 - pair, k]
        return copy(4, piece, piece, k, across)

    def share_mate(k, which):
        piece = panels.at[core, which, k]
        return copy(5, piece, piece, which * chips + k, mate)

    def shared_mate(k, which):
        piece = panels.at[1 - core, which, k]
        return copy(5, piece, piece, which * chips + k, mate)

    own[...] = filtered.reshape(own.shape)
    row = rot_ref[...].astype(jnp.float32)
    lane = lax.broadcasted_iota(jnp.int32, row.shape, 1)
    weight = [jnp.sum(jnp.where(lane == panel, row, 0.0), axis=1, keepdims=True)[None] for panel in range(STEPS)]

    def masked(panel, k):
        return jnp.where(owner_ref[panel] == orb, own[k], 0.0)

    far_first = near[::-1] + [0]
    for step in far_first:
        k = chunk_of(step)
        for which in range(2):
            give[which, k] = masked(2 * which + 1 - core, k)
        to_mate(k).start()
    for step in far_first:
        k = chunk_of(step)
        to_mate(k).wait_recv()
        give_pair[k] = got_core[1 - pair, k] + masked(2 * (1 - pair) + core, k)
        to_across(k).start()
    for step in far_first:
        k = chunk_of(step)
        to_across(k).wait_recv()
        part = got_core[pair, k] + masked(2 * pair + core, k) + got_pair[k]
        if step == 0:
            got_z[z] = part
        else:
            give_z[k] = part
            scatter(k).start()
    for step in near:
        scattered(chunk_of(step)).wait_recv()
    total = got_z[0]
    for k in range(1, chips):
        total = total + got_z[k]
    panels[core, pair, z] = total
    for step in near[::-1]:
        gather(chunk_of(step)).start()
    for step in [0] + near:
        k = chunk_of(step)
        if step != 0:
            gathered(k).wait_recv()
        share_across(k).start()
        share_mate(k, pair).start()
    for step in [0] + near:
        k = chunk_of(step)
        shared_across(k).wait_recv()
        share_mate(k, 1 - pair).start()
    for step in [0] + near:
        k = chunk_of(step)
        shared_mate(k, pair).wait_recv()
        shared_mate(k, 1 - pair).wait_recv()
        rotated_ref[k] = (weight[0] * panels[0, 0, k] + weight[1] * panels[1, 0, k]
                          + weight[2] * panels[0, 1, k] + weight[3] * panels[1, 1, k])
    for step in [0] + near:
        k = chunk_of(step)
        to_mate(k).wait_send()
        to_across(k).wait_send()
        if step != 0:
            scatter(k).wait_send()
            gather(k).wait_send()
        share_across(k).wait_send()
        share_mate(k, pair).wait_send()
        share_mate(k, 1 - pair).wait_send()


def filter_kernel(width, orb_ref, pot_ref, degree_ref, owner_ref, rot_ref, ymat_ref, pmat_ref,
                  out_ref, rotated_ref, field, inner, diag, send_sem, recv_sem, pot_send, pot_recv,
                  hand_send, hand_recv, go_sem, *rotation_scratch):
    count = lax.axis_size("dom")
    me = lax.axis_index("dom")
    has_left = me > 0
    has_right = me < count - 1
    half = RADIUS
    w = width

    def to_left(src, dst, ssem, rsem):
        return pltpu.make_async_remote_copy(
            src_ref=src, dst_ref=dst, send_sem=ssem, recv_sem=rsem,
            device_id={"dom": jnp.maximum(me - 1, 0)}, device_id_type=MESH)

    def to_right(src, dst, ssem, rsem):
        return pltpu.make_async_remote_copy(
            src_ref=src, dst_ref=dst, send_sem=ssem, recv_sem=rsem,
            device_id={"dom": jnp.minimum(me + 1, count - 1)}, device_id_type=MESH)

    def copies(r):
        src = field.at[r, pl.ds(w, w)]
        left = to_left(src, field.at[r, pl.ds(2 * w, w)], send_sem.at[r, 0], recv_sem.at[r, 0])
        right = to_right(src, field.at[r, pl.ds(0, w)], send_sem.at[r, 1], recv_sem.at[r, 1])
        return left, right

    z, pair, core = seat()
    mate = at(z, pair, 1 - core)
    is_first = core == 0
    is_second = core == 1
    low_half, high_half = pl.ds(0, half), pl.ds(half + w, half)
    pot_left = lambda: to_left(pot_ref.at[pl.ds(0, half)], diag.at[high_half], pot_send.at[0], pot_recv.at[0])
    pot_right = lambda: to_right(pot_ref.at[pl.ds(w - half, half)], diag.at[low_half], pot_send.at[1], pot_recv.at[1])

    def hand(side):
        part = diag.at[high_half if side else low_half]
        return pltpu.make_async_remote_copy(
            src_ref=part, dst_ref=part, send_sem=hand_send.at[side], recv_sem=hand_recv.at[side],
            device_id=mate, device_id_type=MESH)

    def on(condition, *actions):
        @pl.when(condition)
        def _():
            for action in actions:
                action()

    peers = [{"dom": lax.rem(me + shift, count)} for shift in (1, count - 1)] + rotation_peers()
    barrier = pltpu.get_barrier_semaphore()
    for peer in peers:
        pl.semaphore_signal(barrier, inc=1, device_id=peer, device_id_type=MESH)
    field[0, w:2 * w] = orb_ref[...].astype(jnp.float32)
    pl.semaphore_wait(barrier, len(peers))

    def start(r):
        on(has_left, lambda: copies(r)[0].start())
        on(has_right, lambda: copies(r)[1].start())

    def sent(r):
        on(has_left, lambda: copies(r)[0].wait_send())
        on(has_right, lambda: copies(r)[1].wait_send())

    def arrive(r):
        on(has_left, lambda: copies(r)[1].wait_recv())
        on(has_right, lambda: copies(r)[0].wait_recv())

    @pl.when(is_first)
    def _():
        start(0)
        sent(0)
        pl.semaphore_signal(go_sem, inc=1, device_id=mate, device_id_type=MESH)

    @pl.when(is_second)
    def _():
        on(has_left, lambda: pot_left().start())
        on(has_right, lambda: pot_right().start())
        pl.semaphore_wait(go_sem, 1)
        start(0)

    @pl.when(jnp.logical_not(has_left))
    def _():
        for r in range(ROUNDS):
            field[r, 0:w] = jnp.zeros((w,) + field.shape[2:], jnp.float32)
        diag[0:half] = jnp.zeros((half,) + diag.shape[1:], jnp.float32)

    @pl.when(jnp.logical_not(has_right))
    def _():
        for r in range(ROUNDS):
            field[r, 2 * w:3 * w] = jnp.zeros((w,) + field.shape[2:], jnp.float32)
        diag[half + w:2 * half + w] = jnp.zeros((half,) + diag.shape[1:], jnp.float32)

    diag[half:half + w] = pot_ref[...]

    @pl.when(is_second)
    def _():
        on(has_left, lambda: pot_right().wait_recv(), lambda: hand(0).start())
        on(has_right, lambda: pot_left().wait_recv(), lambda: hand(1).start())

    @pl.when(is_first)
    def _():
        on(has_left, lambda: hand(0).wait_recv())
        on(has_right, lambda: hand(1).wait_recv())

    planes, cells = field.shape[2], field.shape[3]
    rows = half * planes
    left_mask = jnp.where(has_left, 1.0, 0.0).astype(jnp.float32)
    right_mask = jnp.where(has_right, 1.0, 0.0).astype(jnp.float32)
    degree = degree_ref[0]

    def applied(ref, low, diag_low):
        centre = ref[pl.ds(low, w)]
        total = (diag[pl.ds(diag_low, w)] * SCALE + CENTRE) * centre
        for offset in range(1, RADIUS + 1):
            total = total + SIDE[offset] * (ref[pl.ds(low + offset, w)] + ref[pl.ds(low - offset, w)])
        flat = centre.reshape(2 * rows, cells)
        high = flat.astype(jnp.bfloat16)
        rest = (flat - high.astype(jnp.float32)).astype(jnp.bfloat16)
        both = jnp.dot(jnp.concatenate([high, rest], axis=1), ymat_ref[...], preferred_element_type=jnp.float32)
        total = total + (both[:, :cells] + both[:, cells:]).reshape(centre.shape)
        stacked = jnp.concatenate([
            jnp.concatenate([high[:rows], high[rows:]], axis=1),
            jnp.concatenate([rest[:rows], rest[rows:]], axis=1)], axis=0)
        both = jnp.dot(pmat_ref[...], stacked, preferred_element_type=jnp.float32)
        both = both[:rows] + both[rows:]
        both = jnp.concatenate([both[:, :cells], both[:, cells:]], axis=0)
        return total + both.reshape(centre.shape)

    for r in range(ROUNDS):
        arrive(r)
        now = field.at[r]
        for part in range(2):
            low = part * w
            advanced = applied(now, low + half, low)
            if r == 0:
                advanced = 0.5 * advanced
            else:
                advanced = advanced - inner[low:low + w]
            if part == 0:
                inner[0:half] = advanced[:half] * left_mask
                inner[half:w] = advanced[half:]
            else:
                inner[w:w + half] = advanced[:half]
                inner[w + half:2 * w] = advanced[half:] * right_mask
        advanced = applied(inner, half, half) - now[w:2 * w]
        if r + 1 < ROUNDS:
            field[r + 1, w:2 * w] = advanced
            start(r + 1)
        before = out_ref[...] if r > 0 else jnp.zeros_like(advanced)
        before = jnp.where(degree == 2 * r + 1, inner[half:half + w], before)
        out_ref[...] = jnp.where(degree == 2 * r + 2, advanced, before)

    rotate(out_ref[...], owner_ref, rot_ref, rotated_ref, *rotation_scratch)

    for r in range(1, ROUNDS):
        sent(r)

    @pl.when(is_second)
    def _():
        sent(0)
        on(has_left, lambda: pot_left().wait_send(), lambda: hand(0).wait_send())
        on(has_right, lambda: pot_right().wait_send(), lambda: hand(1).wait_send())


def filter_and_rotate(orbitals, potential, degree, owners, coefficients):
    width, planes, cells = orbitals.shape
    chips = lax.axis_size("orb") // 4
    piece = (width * planes // 8 // chips, 8, cells)
    ymat, pmat = stencil_matrices(planes, cells, RADIUS)
    vmem = pl.BlockSpec(memory_space=pltpu.VMEM)
    smem = pl.BlockSpec(memory_space=pltpu.SMEM)
    buffer = lambda *lead: pltpu.VMEM(lead + piece, jnp.float32)
    filtered, rotated = pl.pallas_call(
        lambda *refs: filter_kernel(width, *refs),
        out_shape=(
            jax.ShapeDtypeStruct(orbitals.shape, jnp.float32),
            jax.ShapeDtypeStruct((chips,) + piece, jnp.float32),
        ),
        in_specs=[vmem, vmem, smem, smem, vmem, vmem, vmem],
        out_specs=(vmem, vmem),
        scratch_shapes=[
            pltpu.VMEM((ROUNDS, 3 * width, planes, cells), jnp.float32),
            pltpu.VMEM((2 * width, planes, cells), jnp.float32),
            pltpu.VMEM((width + 2 * RADIUS, planes, cells), jnp.float32),
            pltpu.SemaphoreType.DMA((ROUNDS, 2)),
            pltpu.SemaphoreType.DMA((ROUNDS, 2)),
            pltpu.SemaphoreType.DMA((2,)),
            pltpu.SemaphoreType.DMA((2,)),
            pltpu.SemaphoreType.DMA((2,)),
            pltpu.SemaphoreType.DMA((2,)),
            pltpu.SemaphoreType.REGULAR,
            buffer(chips), buffer(2, chips), buffer(2, chips), buffer(chips), buffer(chips),
            buffer(chips), buffer(chips), buffer(2, 2, chips),
            pltpu.SemaphoreType.DMA((6, 2, 2 * chips)),
        ],
        compiler_params=pltpu.CompilerParams(collective_id=0, has_side_effects=True),
        name="filter_rotate",
    )(orbitals, potential, degree, owners, coefficients, jnp.asarray(ymat), jnp.asarray(pmat))
    return filtered, rotated.reshape(orbitals.shape)


def per_device(orbitals, potential, degree, owners, rotation):
    layers = jnp.transpose(orbitals[0], (1, 0, 2))
    filtered, rotated = filter_and_rotate(
        layers, jnp.transpose(potential, (1, 0, 2)), degree, owners,
        rotation.reshape(1, STEPS))
    return jnp.transpose(filtered, (1, 0, 2))[None], jnp.transpose(rotated, (1, 0, 2))[None]


def solution(mesh):
    placed = (
        P("orb", None, "dom", None),
        P(None, "dom", None),
        P("orb"),
        P(),
        P(None, None, "orb"),
    )
    return jax.shard_map(
        per_device,
        mesh=mesh,
        in_specs=placed,
        out_specs=(P("orb", None, "dom", None), P("orb", None, "dom", None)),
        check_vma=False,
    )
```

```python
import jax
import jax.numpy as jnp
import numpy as np
from jax import lax
from jax.experimental import pallas as pl
from jax.experimental.pallas import tpu as pltpu
from jax.sharding import PartitionSpec as P

RADIUS = 6
MAXDEG = 8
STEPS = 4
ROUNDS = 4
STENCIL = (
    -5369.0 / 1800.0,
    12.0 / 7.0,
    -15.0 / 56.0,
    10.0 / 189.0,
    -1.0 / 112.0,
    2.0 / 1925.0,
    -1.0 / 16632.0,
)
FILTER_CENTER = 7.75
FILTER_HALF = 6.25
SCALE = 2.0 / FILTER_HALF
MESH = pl.DeviceIdType.MESH

SIDE = [-0.5 * SCALE * c for c in STENCIL]
CENTRE = 3.0 * SIDE[0] - SCALE * FILTER_CENTER


def circulant(size):
    matrix = np.zeros((size, size), np.float64)
    for offset in range(1, RADIUS + 1):
        for index in range(size):
            matrix[index, (index + offset) % size] += SIDE[offset]
            matrix[index, (index - offset) % size] += SIDE[offset]
    return matrix


def halves(matrix):
    high = matrix.astype(jnp.bfloat16)
    low = (matrix - high.astype(np.float64)).astype(jnp.bfloat16)
    return high, low


def stencil_matrices(planes, cells, layers):
    high, low = halves(circulant(cells))
    along_y = np.block([[high, low], [high, low]])
    high, low = halves(np.kron(np.eye(layers), circulant(planes)))
    along_p = np.block([[high, high], [low, low]])
    return along_y, along_p


def seat():
    orb = lax.axis_index("orb")
    return orb // 4, lax.rem(orb // 2, 2), lax.rem(orb, 2)


def at(z, pair, core):
    return {"orb": z * 4 + pair * 2 + core}


def by_distance(chips):
    return sorted(range(1, chips), key=lambda step: (min(step, chips - step), step))


def rotation_peers():
    chips = lax.axis_size("orb") // 4
    z, pair, core = seat()
    return [at(z, pair, 1 - core), at(z, 1 - pair, core)] + [
        at(lax.rem(z + step, chips), pair, core) for step in by_distance(chips)]


def rotate(filtered, owner_ref, rot_ref, rotated_ref, own, give, got_core, give_z, got_z, give_pair,
           got_pair, panels, sems):
    chips = lax.axis_size("orb") // 4
    z, pair, core = seat()
    orb = lax.axis_index("orb")
    near = by_distance(chips)
    chunk_of = lambda step: lax.rem(z + step, chips)
    mate, across = at(z, pair, 1 - core), at(z, 1 - pair, core)

    def copy(stage, src, dst, slot, peer, landing=None):
        return pltpu.make_async_remote_copy(
            src_ref=src, dst_ref=dst, send_sem=sems.at[stage, 0, slot],
            recv_sem=sems.at[stage, 1, slot if landing is None else landing],
            device_id=peer, device_id_type=MESH)

    def to_mate(k):
        return copy(0, give.at[k], got_core.at[k], k, mate)

    def scatter(k):
        return copy(1, give_z.at[k], got_z.at[z], k, at(k, pair, core), z)

    def scattered(k):
        return copy(1, give_z.at[k], got_z.at[k], k, at(k, pair, core))

    def to_across():
        return copy(2, give_pair, got_pair, 0, across)

    def gather(k):
        piece = panels.at[core, z]
        return copy(3, piece, piece, k, at(k, pair, core), z)

    def gathered(k):
        piece = panels.at[core, k]
        return copy(3, piece, piece, k, at(k, pair, core))

    def share(k):
        piece = panels.at[core, k]
        return copy(4, piece, piece, k, mate)

    def shared(k):
        piece = panels.at[1 - core, k]
        return copy(4, piece, piece, k, mate)

    own[...] = filtered.reshape(own.shape)
    row = rot_ref[...].astype(jnp.float32)
    lane = lax.broadcasted_iota(jnp.int32, row.shape, 1)
    weight = [jnp.sum(jnp.where(lane == panel, row, 0.0), axis=1, keepdims=True)[None] for panel in range(STEPS)]

    def masked(panel, k):
        return jnp.where(owner_ref[panel] == orb, own[k], 0.0)

    far_first = near[::-1] + [0]
    for step in far_first:
        k = chunk_of(step)
        for which in range(2):
            give[k, which] = masked(2 * which + 1 - core, k)
        to_mate(k).start()
    for step in far_first:
        k = chunk_of(step)
        to_mate(k).wait_recv()
        target = got_z if step == 0 else give_z
        for which in range(2):
            target[k, which] = got_core[k, which] + masked(2 * which + core, k)
        if step != 0:
            scatter(k).start()
    for step in near:
        scattered(chunk_of(step)).wait_recv()
    total = got_z[0]
    for k in range(1, chips):
        total = total + got_z[k]
    give_pair[...] = total
    to_across().start()
    to_across().wait_recv()
    panels[core, z] = give_pair[...] + got_pair[...]
    for step in near[::-1]:
        gather(chunk_of(step)).start()
    for step in [0] + near:
        k = chunk_of(step)
        if step != 0:
            gathered(k).wait_recv()
        share(k).start()
    for step in [0] + near:
        k = chunk_of(step)
        shared(k).wait_recv()
        rotated_ref[k] = (weight[0] * panels[0, k, 0] + weight[1] * panels[1, k, 0]
                          + weight[2] * panels[0, k, 1] + weight[3] * panels[1, k, 1])
    for step in [0] + near:
        k = chunk_of(step)
        to_mate(k).wait_send()
        if step != 0:
            scatter(k).wait_send()
            gather(k).wait_send()
        share(k).wait_send()
    to_across().wait_send()


def filter_kernel(width, orb_ref, pot_ref, degree_ref, owner_ref, rot_ref, ymat_ref, pmat_ref,
                  out_ref, rotated_ref, field, inner, diag, send_sem, recv_sem, pot_send, pot_recv,
                  hand_send, hand_recv, go_sem, *rotation_scratch):
    count = lax.axis_size("dom")
    me = lax.axis_index("dom")
    has_left = me > 0
    has_right = me < count - 1
    half = RADIUS
    w = width

    def to_left(src, dst, ssem, rsem):
        return pltpu.make_async_remote_copy(
            src_ref=src, dst_ref=dst, send_sem=ssem, recv_sem=rsem,
            device_id={"dom": jnp.maximum(me - 1, 0)}, device_id_type=MESH)

    def to_right(src, dst, ssem, rsem):
        return pltpu.make_async_remote_copy(
            src_ref=src, dst_ref=dst, send_sem=ssem, recv_sem=rsem,
            device_id={"dom": jnp.minimum(me + 1, count - 1)}, device_id_type=MESH)

    def copies(r):
        src = field.at[r, pl.ds(w, w)]
        left = to_left(src, field.at[r, pl.ds(2 * w, w)], send_sem.at[r, 0], recv_sem.at[r, 0])
        right = to_right(src, field.at[r, pl.ds(0, w)], send_sem.at[r, 1], recv_sem.at[r, 1])
        return left, right

    z, pair, core = seat()
    mate = at(z, pair, 1 - core)
    is_first = core == 0
    is_second = core == 1
    low_half, high_half = pl.ds(0, half), pl.ds(half + w, half)
    pot_left = lambda: to_left(pot_ref.at[pl.ds(0, half)], diag.at[high_half], pot_send.at[0], pot_recv.at[0])
    pot_right = lambda: to_right(pot_ref.at[pl.ds(w - half, half)], diag.at[low_half], pot_send.at[1], pot_recv.at[1])

    def hand(side):
        part = diag.at[high_half if side else low_half]
        return pltpu.make_async_remote_copy(
            src_ref=part, dst_ref=part, send_sem=hand_send.at[side], recv_sem=hand_recv.at[side],
            device_id=mate, device_id_type=MESH)

    def on(condition, *actions):
        @pl.when(condition)
        def _():
            for action in actions:
                action()

    peers = [{"dom": lax.rem(me + shift, count)} for shift in (1, count - 1)] + rotation_peers()
    barrier = pltpu.get_barrier_semaphore()
    for peer in peers:
        pl.semaphore_signal(barrier, inc=1, device_id=peer, device_id_type=MESH)
    field[0, w:2 * w] = orb_ref[...].astype(jnp.float32)
    pl.semaphore_wait(barrier, len(peers))

    def start(r):
        on(has_left, lambda: copies(r)[0].start())
        on(has_right, lambda: copies(r)[1].start())

    def sent(r):
        on(has_left, lambda: copies(r)[0].wait_send())
        on(has_right, lambda: copies(r)[1].wait_send())

    def arrive(r):
        on(has_left, lambda: copies(r)[1].wait_recv())
        on(has_right, lambda: copies(r)[0].wait_recv())

    @pl.when(is_first)
    def _():
        start(0)
        sent(0)
        pl.semaphore_signal(go_sem, inc=1, device_id=mate, device_id_type=MESH)

    @pl.when(is_second)
    def _():
        on(has_left, lambda: pot_left().start())
        on(has_right, lambda: pot_right().start())
        pl.semaphore_wait(go_sem, 1)
        start(0)

    @pl.when(jnp.logical_not(has_left))
    def _():
        for r in range(ROUNDS):
            field[r, 0:w] = jnp.zeros((w,) + field.shape[2:], jnp.float32)
        diag[0:half] = jnp.zeros((half,) + diag.shape[1:], jnp.float32)

    @pl.when(jnp.logical_not(has_right))
    def _():
        for r in range(ROUNDS):
            field[r, 2 * w:3 * w] = jnp.zeros((w,) + field.shape[2:], jnp.float32)
        diag[half + w:2 * half + w] = jnp.zeros((half,) + diag.shape[1:], jnp.float32)

    diag[half:half + w] = pot_ref[...]

    @pl.when(is_second)
    def _():
        on(has_left, lambda: pot_right().wait_recv(), lambda: hand(0).start())
        on(has_right, lambda: pot_left().wait_recv(), lambda: hand(1).start())

    @pl.when(is_first)
    def _():
        on(has_left, lambda: hand(0).wait_recv())
        on(has_right, lambda: hand(1).wait_recv())

    planes, cells = field.shape[2], field.shape[3]
    rows = half * planes
    left_mask = jnp.where(has_left, 1.0, 0.0).astype(jnp.float32)
    right_mask = jnp.where(has_right, 1.0, 0.0).astype(jnp.float32)
    degree = degree_ref[0]

    def along_yp(centre):
        flat = centre.reshape(2 * rows, cells)
        high = flat.astype(jnp.bfloat16)
        rest = (flat - high.astype(jnp.float32)).astype(jnp.bfloat16)
        both = jnp.dot(jnp.concatenate([high, rest], axis=1), ymat_ref[...], preferred_element_type=jnp.float32)
        total = both[:, :cells] + both[:, cells:]
        stacked = jnp.concatenate([
            jnp.concatenate([high[:rows], high[rows:]], axis=1),
            jnp.concatenate([rest[:rows], rest[rows:]], axis=1)], axis=0)
        both = jnp.dot(pmat_ref[...], stacked, preferred_element_type=jnp.float32)
        both = both[:rows] + both[rows:]
        both = jnp.concatenate([both[:, :cells], both[:, cells:]], axis=0)
        return (total + both).reshape(centre.shape)

    def along_x(ref, low, diag_low, layers):
        total = (diag[diag_low:diag_low + layers] * SCALE + CENTRE) * ref[low:low + layers]
        for offset in range(1, RADIUS + 1):
            total = total + SIDE[offset] * (
                ref[low + offset:low + offset + layers] + ref[low - offset:low - offset + layers])
        return total

    for r in range(ROUNDS):
        now = field.at[r]
        own_part = along_yp(now[w:2 * w])
        arrive(r)
        halo_part = along_yp(jnp.concatenate([now[w - half:w], now[2 * w:2 * w + half]], axis=0))
        strips = (
            (0, half, halo_part[:half], left_mask),
            (half, w, own_part, None),
            (half + w, half, halo_part[half:], right_mask),
        )
        for low, layers, part, mask in strips:
            advanced = along_x(now, low + half, low, layers) + part
            advanced = 0.5 * advanced if r == 0 else advanced - inner[low:low + layers]
            inner[low:low + layers] = advanced if mask is None else advanced * mask
        advanced = along_x(inner, half, half, w) + along_yp(inner[half:half + w]) - now[w:2 * w]
        if r + 1 < ROUNDS:
            field[r + 1, w:2 * w] = advanced
            start(r + 1)
        before = out_ref[...] if r > 0 else jnp.zeros_like(advanced)
        before = jnp.where(degree == 2 * r + 1, inner[half:half + w], before)
        out_ref[...] = jnp.where(degree == 2 * r + 2, advanced, before)

    rotate(out_ref[...], owner_ref, rot_ref, rotated_ref, *rotation_scratch)

    for r in range(1, ROUNDS):
        sent(r)

    @pl.when(is_second)
    def _():
        sent(0)
        on(has_left, lambda: pot_left().wait_send(), lambda: hand(0).wait_send())
        on(has_right, lambda: pot_right().wait_send(), lambda: hand(1).wait_send())


def filter_and_rotate(orbitals, potential, degree, owners, coefficients):
    width, planes, cells = orbitals.shape
    chips = lax.axis_size("orb") // 4
    piece = (width * planes // 8 // chips, 8, cells)
    ymat, pmat = stencil_matrices(planes, cells, RADIUS)
    vmem = pl.BlockSpec(memory_space=pltpu.VMEM)
    smem = pl.BlockSpec(memory_space=pltpu.SMEM)
    buffer = lambda *lead: pltpu.VMEM(lead + piece, jnp.float32)
    filtered, rotated = pl.pallas_call(
        lambda *refs: filter_kernel(width, *refs),
        out_shape=(
            pltpu.VMEM(orbitals.shape, jnp.float32),
            pltpu.VMEM((chips,) + piece, jnp.float32),
        ),
        in_specs=[vmem, vmem, smem, smem, vmem, vmem, vmem],
        out_specs=(vmem, vmem),
        scratch_shapes=[
            pltpu.VMEM((ROUNDS, 3 * width, planes, cells), jnp.float32),
            pltpu.VMEM((2 * width, planes, cells), jnp.float32),
            pltpu.VMEM((width + 2 * RADIUS, planes, cells), jnp.float32),
            pltpu.SemaphoreType.DMA((ROUNDS, 2)),
            pltpu.SemaphoreType.DMA((ROUNDS, 2)),
            pltpu.SemaphoreType.DMA((2,)),
            pltpu.SemaphoreType.DMA((2,)),
            pltpu.SemaphoreType.DMA((2,)),
            pltpu.SemaphoreType.DMA((2,)),
            pltpu.SemaphoreType.REGULAR,
            buffer(chips), buffer(chips, 2), buffer(chips, 2), buffer(chips, 2), buffer(chips, 2),
            buffer(2), buffer(2), buffer(2, chips, 2),
            pltpu.SemaphoreType.DMA((5, 2, chips)),
        ],
        compiler_params=pltpu.CompilerParams(collective_id=0, has_side_effects=True),
        name="filter_rotate",
    )(orbitals, potential, degree, owners, coefficients, jnp.asarray(ymat), jnp.asarray(pmat))
    return filtered, rotated.reshape(orbitals.shape)


def per_device(orbitals, potential, degree, owners, rotation):
    layers = jnp.transpose(orbitals[0], (1, 0, 2))
    filtered, rotated = filter_and_rotate(
        layers, jnp.transpose(potential, (1, 0, 2)), degree, owners,
        rotation.reshape(1, STEPS))
    return jnp.transpose(filtered, (1, 0, 2))[None], jnp.transpose(rotated, (1, 0, 2))[None]


def solution(mesh):
    placed = (
        P("orb", None, "dom", None),
        P(None, "dom", None),
        P("orb"),
        P(),
        P(None, None, "orb"),
    )
    return jax.shard_map(
        per_device,
        mesh=mesh,
        in_specs=placed,
        out_specs=(P("orb", None, "dom", None), P("orb", None, "dom", None)),
        check_vma=False,
    )
```

```python
import jax
import jax.numpy as jnp
import numpy as np
from jax import lax
from jax.experimental import pallas as pl
from jax.experimental.pallas import tpu as pltpu
from jax.sharding import PartitionSpec as P

RADIUS = 6
MAXDEG = 8
STEPS = 4
ROUNDS = 4
STENCIL = (
    -5369.0 / 1800.0,
    12.0 / 7.0,
    -15.0 / 56.0,
    10.0 / 189.0,
    -1.0 / 112.0,
    2.0 / 1925.0,
    -1.0 / 16632.0,
)
FILTER_CENTER = 7.75
FILTER_HALF = 6.25
SCALE = 2.0 / FILTER_HALF
MESH = pl.DeviceIdType.MESH

SIDE = [-0.5 * SCALE * c for c in STENCIL]
CENTRE = 3.0 * SIDE[0] - SCALE * FILTER_CENTER


def circulant(size):
    matrix = np.zeros((size, size), np.float64)
    for offset in range(1, RADIUS + 1):
        for index in range(size):
            matrix[index, (index + offset) % size] += SIDE[offset]
            matrix[index, (index - offset) % size] += SIDE[offset]
    return matrix


def halves(matrix):
    high = matrix.astype(jnp.bfloat16)
    low = (matrix - high.astype(np.float64)).astype(jnp.bfloat16)
    return high, low


def stencil_matrices(planes, cells, layers):
    high, low = halves(circulant(cells))
    along_y = np.block([[high, low], [high, low]])
    high, low = halves(np.kron(np.eye(layers), circulant(planes)))
    along_p = np.block([[high, high], [low, low]])
    return along_y, along_p


def seat():
    orb = lax.axis_index("orb")
    return orb // 4, lax.rem(orb // 2, 2), lax.rem(orb, 2)


def at(z, pair, core):
    return {"orb": z * 4 + pair * 2 + core}


def by_distance(chips):
    return sorted(range(1, chips), key=lambda step: (min(step, chips - step), step))


def rotation_peers():
    chips = lax.axis_size("orb") // 4
    z, pair, core = seat()
    return [at(z, pair, 1 - core), at(z, 1 - pair, core)] + [
        at(lax.rem(z + step, chips), pair, core) for step in by_distance(chips) if step in (1, chips - 1)]


def vouch(hop, sems):
    chips = lax.axis_size("orb") // 4
    z, pair, core = seat()
    for way, most in ((1, chips // 2 - 1), (chips - 1, (chips - 1) // 2 - 1)):
        side = 0 if way == 1 else 1
        if 2 <= hop <= most + 1:
            pl.semaphore_wait(sems.at[side, hop - 2], 1)
        if hop <= most:
            pl.semaphore_signal(
                sems.at[side, hop - 1], inc=1, device_id=at(lax.rem(z + way, chips), pair, core),
                device_id_type=MESH)


def rotate(filtered, owner_ref, rot_ref, rotated_ref, own, give, got_core, give_z, got_z, give_pair,
           got_pair, panels, sems):
    chips = lax.axis_size("orb") // 4
    z, pair, core = seat()
    orb = lax.axis_index("orb")
    near = by_distance(chips)
    chunk_of = lambda step: lax.rem(z + step, chips)
    mate, across = at(z, pair, 1 - core), at(z, 1 - pair, core)

    def copy(stage, src, dst, slot, peer, landing=None):
        return pltpu.make_async_remote_copy(
            src_ref=src, dst_ref=dst, send_sem=sems.at[stage, 0, slot],
            recv_sem=sems.at[stage, 1, slot if landing is None else landing],
            device_id=peer, device_id_type=MESH)

    def to_mate(k):
        return copy(0, give.at[k], got_core.at[k], k, mate)

    def scatter(k):
        return copy(1, give_z.at[k], got_z.at[z], k, at(k, pair, core), z)

    def scattered(k):
        return copy(1, give_z.at[k], got_z.at[k], k, at(k, pair, core))

    def to_across():
        return copy(2, give_pair, got_pair, 0, across)

    def gather(k):
        piece = panels.at[core, z]
        return copy(3, piece, piece, k, at(k, pair, core), z)

    def gathered(k):
        piece = panels.at[core, k]
        return copy(3, piece, piece, k, at(k, pair, core))

    def share(k):
        piece = panels.at[core, k]
        return copy(4, piece, piece, k, mate)

    def shared(k):
        piece = panels.at[1 - core, k]
        return copy(4, piece, piece, k, mate)

    own[...] = filtered.reshape(own.shape)
    row = rot_ref[...].astype(jnp.float32)
    lane = lax.broadcasted_iota(jnp.int32, row.shape, 1)
    weight = [jnp.sum(jnp.where(lane == panel, row, 0.0), axis=1, keepdims=True)[None] for panel in range(STEPS)]

    def masked(panel, k):
        return jnp.where(owner_ref[panel] == orb, own[k], 0.0)

    far_first = near[::-1] + [0]
    for step in far_first:
        k = chunk_of(step)
        for which in range(2):
            give[k, which] = masked(2 * which + 1 - core, k)
        to_mate(k).start()
    for step in far_first:
        k = chunk_of(step)
        to_mate(k).wait_recv()
        target = got_z if step == 0 else give_z
        for which in range(2):
            target[k, which] = got_core[k, which] + masked(2 * which + core, k)
        if step != 0:
            scatter(k).start()
    for step in near:
        scattered(chunk_of(step)).wait_recv()
    total = got_z[0]
    for k in range(1, chips):
        total = total + got_z[k]
    give_pair[...] = total
    to_across().start()
    to_across().wait_recv()
    panels[core, z] = give_pair[...] + got_pair[...]
    for step in near[::-1]:
        gather(chunk_of(step)).start()
    for step in [0] + near:
        k = chunk_of(step)
        if step != 0:
            gathered(k).wait_recv()
        share(k).start()
    for step in [0] + near:
        k = chunk_of(step)
        shared(k).wait_recv()
        rotated_ref[k] = (weight[0] * panels[0, k, 0] + weight[1] * panels[1, k, 0]
                          + weight[2] * panels[0, k, 1] + weight[3] * panels[1, k, 1])
    for step in [0] + near:
        k = chunk_of(step)
        to_mate(k).wait_send()
        if step != 0:
            scatter(k).wait_send()
            gather(k).wait_send()
        share(k).wait_send()
    to_across().wait_send()


def filter_kernel(width, orb_hbm, pot_hbm, degree_ref, owner_ref, rot_ref, ymat_hbm, pmat_hbm,
                  out_ref, rotated_ref, field, inner, diag, send_sem, recv_sem, pot_send, pot_recv,
                  hand_send, hand_recv, go_sem, vouch_sem, load_sem, orb_ref, pot_ref, ymat_ref,
                  pmat_ref, *rotation_scratch):
    count = lax.axis_size("dom")
    me = lax.axis_index("dom")
    has_left = me > 0
    has_right = me < count - 1
    half = RADIUS
    w = width

    def to_left(src, dst, ssem, rsem):
        return pltpu.make_async_remote_copy(
            src_ref=src, dst_ref=dst, send_sem=ssem, recv_sem=rsem,
            device_id={"dom": jnp.maximum(me - 1, 0)}, device_id_type=MESH)

    def to_right(src, dst, ssem, rsem):
        return pltpu.make_async_remote_copy(
            src_ref=src, dst_ref=dst, send_sem=ssem, recv_sem=rsem,
            device_id={"dom": jnp.minimum(me + 1, count - 1)}, device_id_type=MESH)

    def copies(r):
        src = field.at[r, pl.ds(w, w)]
        left = to_left(src, field.at[r, pl.ds(2 * w, w)], send_sem.at[r, 0], recv_sem.at[r, 0])
        right = to_right(src, field.at[r, pl.ds(0, w)], send_sem.at[r, 1], recv_sem.at[r, 1])
        return left, right

    z, pair, core = seat()
    mate = at(z, pair, 1 - core)
    is_first = core == 0
    is_second = core == 1
    low_half, high_half = pl.ds(0, half), pl.ds(half + w, half)
    pot_left = lambda: to_left(pot_ref.at[pl.ds(0, half)], diag.at[high_half], pot_send.at[0], pot_recv.at[0])
    pot_right = lambda: to_right(pot_ref.at[pl.ds(w - half, half)], diag.at[low_half], pot_send.at[1], pot_recv.at[1])

    def hand(side):
        part = diag.at[high_half if side else low_half]
        return pltpu.make_async_remote_copy(
            src_ref=part, dst_ref=part, send_sem=hand_send.at[side], recv_sem=hand_recv.at[side],
            device_id=mate, device_id_type=MESH)

    def on(condition, *actions):
        @pl.when(condition)
        def _():
            for action in actions:
                action()

    peers = [{"dom": lax.rem(me + shift, count)} for shift in (1, count - 1)] + rotation_peers()
    barrier = pltpu.get_barrier_semaphore()
    for peer in peers:
        pl.semaphore_signal(barrier, inc=1, device_id=peer, device_id_type=MESH)
    loads = [
        pltpu.make_async_copy(src, dst, load_sem.at[slot])
        for slot, (src, dst) in enumerate((
            (orb_hbm, orb_ref), (pot_hbm, pot_ref), (ymat_hbm, ymat_ref), (pmat_hbm, pmat_ref)))]
    for load in loads:
        load.start()
    loads[0].wait()
    field[0, w:2 * w] = orb_ref[...].astype(jnp.float32)
    loads[1].wait()
    pl.semaphore_wait(barrier, len(peers))

    def start(r):
        on(has_left, lambda: copies(r)[0].start())
        on(has_right, lambda: copies(r)[1].start())

    def sent(r):
        on(has_left, lambda: copies(r)[0].wait_send())
        on(has_right, lambda: copies(r)[1].wait_send())

    def arrive(r):
        on(has_left, lambda: copies(r)[1].wait_recv())
        on(has_right, lambda: copies(r)[0].wait_recv())

    @pl.when(is_first)
    def _():
        start(0)
        sent(0)
        pl.semaphore_signal(go_sem, inc=1, device_id=mate, device_id_type=MESH)

    @pl.when(is_second)
    def _():
        on(has_left, lambda: pot_left().start())
        on(has_right, lambda: pot_right().start())
        pl.semaphore_wait(go_sem, 1)
        start(0)

    @pl.when(jnp.logical_not(has_left))
    def _():
        for r in range(ROUNDS):
            field[r, 0:w] = jnp.zeros((w,) + field.shape[2:], jnp.float32)
        diag[0:half] = jnp.zeros((half,) + diag.shape[1:], jnp.float32)

    @pl.when(jnp.logical_not(has_right))
    def _():
        for r in range(ROUNDS):
            field[r, 2 * w:3 * w] = jnp.zeros((w,) + field.shape[2:], jnp.float32)
        diag[half + w:2 * half + w] = jnp.zeros((half,) + diag.shape[1:], jnp.float32)

    diag[half:half + w] = pot_ref[...]
    loads[2].wait()
    loads[3].wait()

    @pl.when(is_second)
    def _():
        on(has_left, lambda: pot_right().wait_recv(), lambda: hand(0).start())
        on(has_right, lambda: pot_left().wait_recv(), lambda: hand(1).start())

    @pl.when(is_first)
    def _():
        on(has_left, lambda: hand(0).wait_recv())
        on(has_right, lambda: hand(1).wait_recv())

    planes, cells = field.shape[2], field.shape[3]
    rows = half * planes
    left_mask = jnp.where(has_left, 1.0, 0.0).astype(jnp.float32)
    right_mask = jnp.where(has_right, 1.0, 0.0).astype(jnp.float32)
    degree = degree_ref[0]

    def along_yp(centre):
        flat = centre.reshape(2 * rows, cells)
        high = flat.astype(jnp.bfloat16)
        rest = (flat - high.astype(jnp.float32)).astype(jnp.bfloat16)
        both = jnp.dot(jnp.concatenate([high, rest], axis=1), ymat_ref[...], preferred_element_type=jnp.float32)
        total = both[:, :cells] + both[:, cells:]
        stacked = jnp.concatenate([
            jnp.concatenate([high[:rows], high[rows:]], axis=1),
            jnp.concatenate([rest[:rows], rest[rows:]], axis=1)], axis=0)
        both = jnp.dot(pmat_ref[...], stacked, preferred_element_type=jnp.float32)
        both = both[:rows] + both[rows:]
        both = jnp.concatenate([both[:, :cells], both[:, cells:]], axis=0)
        return (total + both).reshape(centre.shape)

    def along_x(ref, low, diag_low, layers):
        total = (diag[diag_low:diag_low + layers] * SCALE + CENTRE) * ref[low:low + layers]
        for offset in range(1, RADIUS + 1):
            total = total + SIDE[offset] * (
                ref[low + offset:low + offset + layers] + ref[low - offset:low - offset + layers])
        return total

    for r in range(ROUNDS):
        now = field.at[r]
        own_part = along_yp(now[w:2 * w])
        arrive(r)
        halo_part = along_yp(jnp.concatenate([now[w - half:w], now[2 * w:2 * w + half]], axis=0))
        strips = (
            (0, half, halo_part[:half], left_mask),
            (half, w, own_part, None),
            (half + w, half, halo_part[half:], right_mask),
        )
        for low, layers, part, mask in strips:
            advanced = along_x(now, low + half, low, layers) + part
            advanced = 0.5 * advanced if r == 0 else advanced - inner[low:low + layers]
            inner[low:low + layers] = advanced if mask is None else advanced * mask
        advanced = along_x(inner, half, half, w) + along_yp(inner[half:half + w]) - now[w:2 * w]
        if r + 1 < ROUNDS:
            field[r + 1, w:2 * w] = advanced
            start(r + 1)
        vouch(r + 1, vouch_sem)
        before = out_ref[...] if r > 0 else jnp.zeros_like(advanced)
        before = jnp.where(degree == 2 * r + 1, inner[half:half + w], before)
        out_ref[...] = jnp.where(degree == 2 * r + 2, advanced, before)

    rotate(out_ref[...], owner_ref, rot_ref, rotated_ref, *rotation_scratch)

    for r in range(1, ROUNDS):
        sent(r)

    @pl.when(is_second)
    def _():
        sent(0)
        on(has_left, lambda: pot_left().wait_send(), lambda: hand(0).wait_send())
        on(has_right, lambda: pot_right().wait_send(), lambda: hand(1).wait_send())


def filter_and_rotate(orbitals, potential, degree, owners, coefficients):
    width, planes, cells = orbitals.shape
    chips = lax.axis_size("orb") // 4
    piece = (width * planes // 8 // chips, 8, cells)
    ymat, pmat = stencil_matrices(planes, cells, RADIUS)
    vmem = pl.BlockSpec(memory_space=pltpu.VMEM)
    smem = pl.BlockSpec(memory_space=pltpu.SMEM)
    hbm = pl.BlockSpec(memory_space=pl.ANY)
    buffer = lambda *lead: pltpu.VMEM(lead + piece, jnp.float32)
    filtered, rotated = pl.pallas_call(
        lambda *refs: filter_kernel(width, *refs),
        out_shape=(
            pltpu.VMEM(orbitals.shape, jnp.float32),
            pltpu.VMEM((chips,) + piece, jnp.float32),
        ),
        in_specs=[hbm, hbm, smem, smem, vmem, hbm, hbm],
        out_specs=(vmem, vmem),
        scratch_shapes=[
            pltpu.VMEM((ROUNDS, 3 * width, planes, cells), jnp.float32),
            pltpu.VMEM((2 * width, planes, cells), jnp.float32),
            pltpu.VMEM((width + 2 * RADIUS, planes, cells), jnp.float32),
            pltpu.SemaphoreType.DMA((ROUNDS, 2)),
            pltpu.SemaphoreType.DMA((ROUNDS, 2)),
            pltpu.SemaphoreType.DMA((2,)),
            pltpu.SemaphoreType.DMA((2,)),
            pltpu.SemaphoreType.DMA((2,)),
            pltpu.SemaphoreType.DMA((2,)),
            pltpu.SemaphoreType.REGULAR,
            pltpu.SemaphoreType.REGULAR((2, ROUNDS)),
            pltpu.SemaphoreType.DMA((4,)),
            pltpu.VMEM(orbitals.shape, orbitals.dtype),
            pltpu.VMEM(potential.shape, jnp.float32),
            pltpu.VMEM(ymat.shape, jnp.bfloat16),
            pltpu.VMEM(pmat.shape, jnp.bfloat16),
            buffer(chips), buffer(chips, 2), buffer(chips, 2), buffer(chips, 2), buffer(chips, 2),
            buffer(2), buffer(2), buffer(2, chips, 2),
            pltpu.SemaphoreType.DMA((5, 2, chips)),
        ],
        compiler_params=pltpu.CompilerParams(collective_id=0, has_side_effects=True),
        name="filter_rotate",
    )(orbitals, potential, degree, owners, coefficients, jnp.asarray(ymat), jnp.asarray(pmat))
    return filtered, rotated.reshape(orbitals.shape)


def per_device(orbitals, potential, degree, owners, rotation):
    layers = jnp.transpose(orbitals[0], (1, 0, 2))
    filtered, rotated = filter_and_rotate(
        layers, jnp.transpose(potential, (1, 0, 2)), degree, owners,
        rotation.reshape(1, STEPS))
    return jnp.transpose(filtered, (1, 0, 2))[None], jnp.transpose(rotated, (1, 0, 2))[None]


def solution(mesh):
    placed = (
        P("orb", None, "dom", None),
        P(None, "dom", None),
        P("orb"),
        P(),
        P(None, None, "orb"),
    )
    return jax.shard_map(
        per_device,
        mesh=mesh,
        in_specs=placed,
        out_specs=(P("orb", None, "dom", None), P("orb", None, "dom", None)),
        check_vma=False,
    )
```

```python
import jax
import jax.numpy as jnp
import numpy as np
from jax import lax
from jax.experimental import pallas as pl
from jax.experimental.pallas import tpu as pltpu
from jax.sharding import PartitionSpec as P

RADIUS = 6
MAXDEG = 8
STEPS = 4
ROUNDS = 4
STENCIL = (
    -5369.0 / 1800.0,
    12.0 / 7.0,
    -15.0 / 56.0,
    10.0 / 189.0,
    -1.0 / 112.0,
    2.0 / 1925.0,
    -1.0 / 16632.0,
)
FILTER_CENTER = 7.75
FILTER_HALF = 6.25
SCALE = 2.0 / FILTER_HALF
MESH = pl.DeviceIdType.MESH

SIDE = [-0.5 * SCALE * c for c in STENCIL]
CENTRE = 3.0 * SIDE[0] - SCALE * FILTER_CENTER


def circulant(size):
    matrix = np.zeros((size, size), np.float64)
    for offset in range(1, RADIUS + 1):
        for index in range(size):
            matrix[index, (index + offset) % size] += SIDE[offset]
            matrix[index, (index - offset) % size] += SIDE[offset]
    return matrix


def halves(matrix):
    high = matrix.astype(jnp.bfloat16)
    low = (matrix - high.astype(np.float64)).astype(jnp.bfloat16)
    return high, low


def stencil_matrices(planes, cells, layers):
    high, low = halves(circulant(cells))
    along_y = np.block([[high, low], [high, low]])
    high, low = halves(np.kron(np.eye(layers), circulant(planes)))
    along_p = np.block([[high, high], [low, low]])
    return along_y, along_p


def seat():
    orb = lax.axis_index("orb")
    return orb // 4, lax.rem(orb // 2, 2), lax.rem(orb, 2)


def at(z, pair, core):
    return {"orb": z * 4 + pair * 2 + core}


def by_distance(chips):
    return sorted(range(1, chips), key=lambda step: (min(step, chips - step), step))


def rotation_peers():
    chips = lax.axis_size("orb") // 4
    z, pair, core = seat()
    return [at(z, pair, 1 - core), at(z, 1 - pair, core)] + [
        at(lax.rem(z + step, chips), pair, core) for step in by_distance(chips) if step in (1, chips - 1)]


def vouch(hop, sems):
    chips = lax.axis_size("orb") // 4
    z, pair, core = seat()
    for way, most in ((1, chips // 2 - 1), (chips - 1, (chips - 1) // 2 - 1)):
        side = 0 if way == 1 else 1
        if 2 <= hop <= most + 1:
            pl.semaphore_wait(sems.at[side, hop - 2], 1)
        if hop <= most:
            pl.semaphore_signal(
                sems.at[side, hop - 1], inc=1, device_id=at(lax.rem(z + way, chips), pair, core),
                device_id_type=MESH)


def rotate(filtered, owner_ref, rot_ref, rotated_ref, own, give, got_core, give_z, got_z, give_pair,
           got_pair, panels, sems):
    chips = lax.axis_size("orb") // 4
    z, pair, core = seat()
    orb = lax.axis_index("orb")
    near = by_distance(chips)
    chunk_of = lambda step: lax.rem(z + step, chips)
    mate, across = at(z, pair, 1 - core), at(z, 1 - pair, core)

    def copy(stage, src, dst, slot, peer, landing=None):
        return pltpu.make_async_remote_copy(
            src_ref=src, dst_ref=dst, send_sem=sems.at[stage, 0, slot],
            recv_sem=sems.at[stage, 1, slot if landing is None else landing],
            device_id=peer, device_id_type=MESH)

    def to_mate(k):
        return copy(0, give.at[k], got_core.at[k], k, mate)

    def scatter(k):
        return copy(1, give_z.at[k], got_z.at[z], k, at(k, pair, core), z)

    def scattered(k):
        return copy(1, give_z.at[k], got_z.at[k], k, at(k, pair, core))

    def to_across():
        return copy(2, give_pair, got_pair, 0, across)

    def gather(k):
        piece = panels.at[core, z]
        return copy(3, piece, piece, k, at(k, pair, core), z)

    def gathered(k):
        piece = panels.at[core, k]
        return copy(3, piece, piece, k, at(k, pair, core))

    def share(k):
        piece = panels.at[core, k]
        return copy(4, piece, piece, k, mate)

    def shared(k):
        piece = panels.at[1 - core, k]
        return copy(4, piece, piece, k, mate)

    own[...] = filtered.reshape(own.shape)
    row = rot_ref[...].astype(jnp.float32)
    lane = lax.broadcasted_iota(jnp.int32, row.shape, 1)
    weight = [jnp.sum(jnp.where(lane == panel, row, 0.0), axis=1, keepdims=True)[None] for panel in range(STEPS)]

    def masked(panel, k):
        return jnp.where(owner_ref[panel] == orb, own[k], 0.0)

    far_first = near[::-1] + [0]
    for step in far_first:
        k = chunk_of(step)
        for which in range(2):
            give[k, which] = masked(2 * which + 1 - core, k)
        to_mate(k).start()
    for step in far_first:
        k = chunk_of(step)
        to_mate(k).wait_recv()
        target = got_z if step == 0 else give_z
        for which in range(2):
            target[k, which] = got_core[k, which] + masked(2 * which + core, k)
        if step != 0:
            scatter(k).start()
    for step in near:
        scattered(chunk_of(step)).wait_recv()
    total = got_z[0]
    for k in range(1, chips):
        total = total + got_z[k]
    give_pair[...] = total
    to_across().start()
    to_across().wait_recv()
    panels[core, z] = give_pair[...] + got_pair[...]
    for step in near[::-1]:
        gather(chunk_of(step)).start()
    for step in [0] + near:
        k = chunk_of(step)
        if step != 0:
            gathered(k).wait_recv()
        share(k).start()
    for step in [0] + near:
        k = chunk_of(step)
        shared(k).wait_recv()
        rotated_ref[k] = (weight[0] * panels[0, k, 0] + weight[1] * panels[1, k, 0]
                          + weight[2] * panels[0, k, 1] + weight[3] * panels[1, k, 1])
    for step in [0] + near:
        k = chunk_of(step)
        to_mate(k).wait_send()
        if step != 0:
            scatter(k).wait_send()
            gather(k).wait_send()
        share(k).wait_send()
    to_across().wait_send()


def filter_kernel(width, orb_hbm, pot_hbm, degree_ref, owner_ref, rot_ref, ymat_hbm, pmat_hbm,
                  result_ref, out_ref, field, inner, diag, send_sem, recv_sem, pot_send, pot_recv,
                  hand_send, hand_recv, go_sem, vouch_sem, load_sem, orb_ref, pot_ref, ymat_ref,
                  pmat_ref, *rotation_scratch):
    count = lax.axis_size("dom")
    me = lax.axis_index("dom")
    has_left = me > 0
    has_right = me < count - 1
    half = RADIUS
    w = width

    def to_left(src, dst, ssem, rsem):
        return pltpu.make_async_remote_copy(
            src_ref=src, dst_ref=dst, send_sem=ssem, recv_sem=rsem,
            device_id={"dom": jnp.maximum(me - 1, 0)}, device_id_type=MESH)

    def to_right(src, dst, ssem, rsem):
        return pltpu.make_async_remote_copy(
            src_ref=src, dst_ref=dst, send_sem=ssem, recv_sem=rsem,
            device_id={"dom": jnp.minimum(me + 1, count - 1)}, device_id_type=MESH)

    def copies(r):
        src = field.at[r, pl.ds(w, w)]
        left = to_left(src, field.at[r, pl.ds(2 * w, w)], send_sem.at[r, 0], recv_sem.at[r, 0])
        right = to_right(src, field.at[r, pl.ds(0, w)], send_sem.at[r, 1], recv_sem.at[r, 1])
        return left, right

    z, pair, core = seat()
    mate = at(z, pair, 1 - core)
    is_first = core == 0
    is_second = core == 1
    low_half, high_half = pl.ds(0, half), pl.ds(half + w, half)
    pot_left = lambda: to_left(pot_ref.at[pl.ds(0, half)], diag.at[high_half], pot_send.at[0], pot_recv.at[0])
    pot_right = lambda: to_right(pot_ref.at[pl.ds(w - half, half)], diag.at[low_half], pot_send.at[1], pot_recv.at[1])

    def hand(side):
        part = diag.at[high_half if side else low_half]
        return pltpu.make_async_remote_copy(
            src_ref=part, dst_ref=part, send_sem=hand_send.at[side], recv_sem=hand_recv.at[side],
            device_id=mate, device_id_type=MESH)

    def on(condition, *actions):
        @pl.when(condition)
        def _():
            for action in actions:
                action()

    peers = [{"dom": lax.rem(me + shift, count)} for shift in (1, count - 1)] + rotation_peers()
    barrier = pltpu.get_barrier_semaphore()
    for peer in peers:
        pl.semaphore_signal(barrier, inc=1, device_id=peer, device_id_type=MESH)
    loads = [
        pltpu.make_async_copy(src, dst, load_sem.at[slot])
        for slot, (src, dst) in enumerate((
            (orb_hbm, orb_ref), (pot_hbm, pot_ref), (ymat_hbm, ymat_ref), (pmat_hbm, pmat_ref)))]
    for load in loads:
        load.start()
    loads[0].wait()
    field[0, w:2 * w] = orb_ref[...].astype(jnp.float32)
    loads[1].wait()
    pl.semaphore_wait(barrier, len(peers))

    def start(r):
        on(has_left, lambda: copies(r)[0].start())
        on(has_right, lambda: copies(r)[1].start())

    def sent(r):
        on(has_left, lambda: copies(r)[0].wait_send())
        on(has_right, lambda: copies(r)[1].wait_send())

    def arrive(r):
        on(has_left, lambda: copies(r)[1].wait_recv())
        on(has_right, lambda: copies(r)[0].wait_recv())

    @pl.when(is_first)
    def _():
        start(0)
        sent(0)
        pl.semaphore_signal(go_sem, inc=1, device_id=mate, device_id_type=MESH)

    @pl.when(is_second)
    def _():
        on(has_left, lambda: pot_left().start())
        on(has_right, lambda: pot_right().start())
        pl.semaphore_wait(go_sem, 1)
        start(0)

    @pl.when(jnp.logical_not(has_left))
    def _():
        for r in range(ROUNDS):
            field[r, 0:w] = jnp.zeros((w,) + field.shape[2:], jnp.float32)
        diag[0:half] = jnp.zeros((half,) + diag.shape[1:], jnp.float32)

    @pl.when(jnp.logical_not(has_right))
    def _():
        for r in range(ROUNDS):
            field[r, 2 * w:3 * w] = jnp.zeros((w,) + field.shape[2:], jnp.float32)
        diag[half + w:2 * half + w] = jnp.zeros((half,) + diag.shape[1:], jnp.float32)

    diag[half:half + w] = pot_ref[...]
    loads[2].wait()
    loads[3].wait()

    @pl.when(is_second)
    def _():
        on(has_left, lambda: pot_right().wait_recv(), lambda: hand(0).start())
        on(has_right, lambda: pot_left().wait_recv(), lambda: hand(1).start())

    @pl.when(is_first)
    def _():
        on(has_left, lambda: hand(0).wait_recv())
        on(has_right, lambda: hand(1).wait_recv())

    planes, cells = field.shape[2], field.shape[3]
    rows = half * planes
    left_mask = jnp.where(has_left, 1.0, 0.0).astype(jnp.float32)
    right_mask = jnp.where(has_right, 1.0, 0.0).astype(jnp.float32)
    degree = degree_ref[0]

    def along_yp(centre):
        flat = centre.reshape(2 * rows, cells)
        high = flat.astype(jnp.bfloat16)
        rest = (flat - high.astype(jnp.float32)).astype(jnp.bfloat16)
        both = jnp.dot(jnp.concatenate([high, rest], axis=1), ymat_ref[...], preferred_element_type=jnp.float32)
        total = both[:, :cells] + both[:, cells:]
        stacked = jnp.concatenate([
            jnp.concatenate([high[:rows], high[rows:]], axis=1),
            jnp.concatenate([rest[:rows], rest[rows:]], axis=1)], axis=0)
        both = jnp.dot(pmat_ref[...], stacked, preferred_element_type=jnp.float32)
        both = both[:rows] + both[rows:]
        both = jnp.concatenate([both[:, :cells], both[:, cells:]], axis=0)
        return (total + both).reshape(centre.shape)

    def along_x(ref, low, diag_low, layers):
        total = (diag[diag_low:diag_low + layers] * SCALE + CENTRE) * ref[low:low + layers]
        for offset in range(1, RADIUS + 1):
            total = total + SIDE[offset] * (
                ref[low + offset:low + offset + layers] + ref[low - offset:low - offset + layers])
        return total

    for r in range(ROUNDS):
        now = field.at[r]
        own_part = along_yp(now[w:2 * w])
        arrive(r)
        halo_part = along_yp(jnp.concatenate([now[w - half:w], now[2 * w:2 * w + half]], axis=0))
        strips = (
            (0, half, halo_part[:half], left_mask),
            (half, w, own_part, None),
            (half + w, half, halo_part[half:], right_mask),
        )
        for low, layers, part, mask in strips:
            advanced = along_x(now, low + half, low, layers) + part
            advanced = 0.5 * advanced if r == 0 else advanced - inner[low:low + layers]
            inner[low:low + layers] = advanced if mask is None else advanced * mask
        advanced = along_x(inner, half, half, w) + along_yp(inner[half:half + w]) - now[w:2 * w]
        if r + 1 < ROUNDS:
            field[r + 1, w:2 * w] = advanced
            start(r + 1)
        vouch(r + 1, vouch_sem)
        before = out_ref[...] if r > 0 else jnp.zeros_like(advanced)
        before = jnp.where(degree == 2 * r + 1, inner[half:half + w], before)
        out_ref[...] = jnp.where(degree == 2 * r + 2, advanced, before)

    result_ref[0] = out_ref[...].reshape(result_ref.shape[1:])
    rotate(out_ref[...], owner_ref, rot_ref, result_ref.at[1], *rotation_scratch)

    for r in range(1, ROUNDS):
        sent(r)

    @pl.when(is_second)
    def _():
        sent(0)
        on(has_left, lambda: pot_left().wait_send(), lambda: hand(0).wait_send())
        on(has_right, lambda: pot_right().wait_send(), lambda: hand(1).wait_send())


def filter_and_rotate(orbitals, potential, degree, owners, coefficients):
    width, planes, cells = orbitals.shape
    chips = lax.axis_size("orb") // 4
    piece = (width * planes // 8 // chips, 8, cells)
    ymat, pmat = stencil_matrices(planes, cells, RADIUS)
    vmem = pl.BlockSpec(memory_space=pltpu.VMEM)
    smem = pl.BlockSpec(memory_space=pltpu.SMEM)
    hbm = pl.BlockSpec(memory_space=pl.ANY)
    buffer = lambda *lead: pltpu.VMEM(lead + piece, jnp.float32)
    result = pl.pallas_call(
        lambda *refs: filter_kernel(width, *refs),
        out_shape=pltpu.VMEM((2, chips) + piece, jnp.float32),
        in_specs=[hbm, hbm, smem, smem, vmem, hbm, hbm],
        out_specs=vmem,
        scratch_shapes=[
            pltpu.VMEM(orbitals.shape, jnp.float32),
            pltpu.VMEM((ROUNDS, 3 * width, planes, cells), jnp.float32),
            pltpu.VMEM((2 * width, planes, cells), jnp.float32),
            pltpu.VMEM((width + 2 * RADIUS, planes, cells), jnp.float32),
            pltpu.SemaphoreType.DMA((ROUNDS, 2)),
            pltpu.SemaphoreType.DMA((ROUNDS, 2)),
            pltpu.SemaphoreType.DMA((2,)),
            pltpu.SemaphoreType.DMA((2,)),
            pltpu.SemaphoreType.DMA((2,)),
            pltpu.SemaphoreType.DMA((2,)),
            pltpu.SemaphoreType.REGULAR,
            pltpu.SemaphoreType.REGULAR((2, ROUNDS)),
            pltpu.SemaphoreType.DMA((4,)),
            pltpu.VMEM(orbitals.shape, orbitals.dtype),
            pltpu.VMEM(potential.shape, jnp.float32),
            pltpu.VMEM(ymat.shape, jnp.bfloat16),
            pltpu.VMEM(pmat.shape, jnp.bfloat16),
            buffer(chips), buffer(chips, 2), buffer(chips, 2), buffer(chips, 2), buffer(chips, 2),
            buffer(2), buffer(2), buffer(2, chips, 2),
            pltpu.SemaphoreType.DMA((5, 2, chips)),
        ],
        compiler_params=pltpu.CompilerParams(collective_id=0, has_side_effects=True),
        name="filter_rotate",
    )(orbitals, potential, degree, owners, coefficients, jnp.asarray(ymat), jnp.asarray(pmat))
    result = result.reshape((2,) + orbitals.shape)
    return result[0], result[1]


def per_device(orbitals, potential, degree, owners, rotation):
    layers = jnp.transpose(orbitals[0], (1, 0, 2))
    filtered, rotated = filter_and_rotate(
        layers, jnp.transpose(potential, (1, 0, 2)), degree, owners,
        rotation.reshape(1, STEPS))
    return jnp.transpose(filtered, (1, 0, 2))[None], jnp.transpose(rotated, (1, 0, 2))[None]


def solution(mesh):
    placed = (
        P("orb", None, "dom", None),
        P(None, "dom", None),
        P("orb"),
        P(),
        P(None, None, "orb"),
    )
    return jax.shard_map(
        per_device,
        mesh=mesh,
        in_specs=placed,
        out_specs=(P("orb", None, "dom", None), P("orb", None, "dom", None)),
        check_vma=False,
    )
```

```python
import jax
import jax.numpy as jnp
import numpy as np
from jax import lax
from jax.experimental import pallas as pl
from jax.experimental.pallas import tpu as pltpu
from jax.sharding import PartitionSpec as P

RADIUS = 6
MAXDEG = 8
STEPS = 4
ROUNDS = 4
STENCIL = (
    -5369.0 / 1800.0,
    12.0 / 7.0,
    -15.0 / 56.0,
    10.0 / 189.0,
    -1.0 / 112.0,
    2.0 / 1925.0,
    -1.0 / 16632.0,
)
FILTER_CENTER = 7.75
FILTER_HALF = 6.25
SCALE = 2.0 / FILTER_HALF
MESH = pl.DeviceIdType.MESH

SIDE = [-0.5 * SCALE * c for c in STENCIL]
CENTRE = 3.0 * SIDE[0] - SCALE * FILTER_CENTER


def circulant(size):
    matrix = np.zeros((size, size), np.float64)
    for offset in range(1, RADIUS + 1):
        for index in range(size):
            matrix[index, (index + offset) % size] += SIDE[offset]
            matrix[index, (index - offset) % size] += SIDE[offset]
    return matrix


def halves(matrix):
    high = matrix.astype(jnp.bfloat16)
    low = (matrix - high.astype(np.float64)).astype(jnp.bfloat16)
    return high, low


def stencil_matrices(planes, cells, layers):
    high, low = halves(circulant(cells))
    along_y = np.block([[high, low], [high, low]])
    high, low = halves(np.kron(np.eye(layers), circulant(planes)))
    along_p = np.block([[high, high], [low, low]])
    return along_y, along_p


def seat():
    orb = lax.axis_index("orb")
    return orb // 4, lax.rem(orb // 2, 2), lax.rem(orb, 2)


def at(z, pair, core):
    return {"orb": z * 4 + pair * 2 + core}


def by_distance(chips):
    return sorted(range(1, chips), key=lambda step: (min(step, chips - step), step))


def rotation_peers():
    chips = lax.axis_size("orb") // 4
    z, pair, core = seat()
    return [at(z, pair, 1 - core), at(z, 1 - pair, core)] + [
        at(lax.rem(z + step, chips), pair, core) for step in by_distance(chips) if step in (1, chips - 1)]


def vouch(hop, sems):
    chips = lax.axis_size("orb") // 4
    z, pair, core = seat()
    for way, most in ((1, chips // 2 - 1), (chips - 1, (chips - 1) // 2 - 1)):
        side = 0 if way == 1 else 1
        if 2 <= hop <= most + 1:
            pl.semaphore_wait(sems.at[side, hop - 2], 1)
        if hop <= most:
            pl.semaphore_signal(
                sems.at[side, hop - 1], inc=1, device_id=at(lax.rem(z + way, chips), pair, core),
                device_id_type=MESH)


def rotate(filtered, owner_ref, rot_ref, rotated_ref, own, give, got_core, give_z, got_z, give_pair,
           got_pair, panels, sems):
    chips = lax.axis_size("orb") // 4
    z, pair, core = seat()
    orb = lax.axis_index("orb")
    near = by_distance(chips)
    chunk_of = lambda step: lax.rem(z + step, chips)
    mate, across = at(z, pair, 1 - core), at(z, 1 - pair, core)

    def copy(stage, src, dst, slot, peer, landing=None):
        return pltpu.make_async_remote_copy(
            src_ref=src, dst_ref=dst, send_sem=sems.at[stage, 0, slot],
            recv_sem=sems.at[stage, 1, slot if landing is None else landing],
            device_id=peer, device_id_type=MESH)

    def to_mate(k):
        return copy(0, give.at[k], got_core.at[k], k, mate)

    def scatter(k):
        return copy(1, give_z.at[k], got_z.at[z], k, at(k, pair, core), z)

    def scattered(k):
        return copy(1, give_z.at[k], got_z.at[k], k, at(k, pair, core))

    def to_across(which):
        return copy(2, give_pair.at[which], got_pair.at[which], which, across)

    def gather(k):
        piece = panels.at[core, z]
        return copy(3, piece, piece, k, at(k, pair, core), z)

    def gathered(k):
        piece = panels.at[core, k]
        return copy(3, piece, piece, k, at(k, pair, core))

    def share(k):
        piece = panels.at[core, k]
        return copy(4, piece, piece, k, mate)

    def shared(k):
        piece = panels.at[1 - core, k]
        return copy(4, piece, piece, k, mate)

    own[...] = filtered.reshape(own.shape)
    row = rot_ref[...].astype(jnp.float32)
    lane = lax.broadcasted_iota(jnp.int32, row.shape, 1)
    weight = [jnp.sum(jnp.where(lane == panel, row, 0.0), axis=1, keepdims=True)[None] for panel in range(STEPS)]

    def masked(panel, k):
        return jnp.where(owner_ref[panel] == orb, own[k], 0.0)

    far_first = near[::-1] + [0]
    for step in far_first:
        k = chunk_of(step)
        for which in range(2):
            give[k, which] = masked(2 * which + 1 - core, k)
        to_mate(k).start()
    for step in far_first:
        k = chunk_of(step)
        to_mate(k).wait_recv()
        target = got_z if step == 0 else give_z
        for which in range(2):
            target[k, which] = got_core[k, which] + masked(2 * which + core, k)
        if step != 0:
            scatter(k).start()
    for step in near:
        scattered(chunk_of(step)).wait_recv()
    for which in range(2):
        total = got_z[0, which]
        for k in range(1, chips):
            total = total + got_z[k, which]
        give_pair[which] = total
        to_across(which).start()
    for which in range(2):
        to_across(which).wait_recv()
        panels[core, z, which] = give_pair[which] + got_pair[which]
    for step in near[::-1]:
        gather(chunk_of(step)).start()
    for step in [0] + near:
        k = chunk_of(step)
        if step != 0:
            gathered(k).wait_recv()
        share(k).start()
    for step in [0] + near:
        k = chunk_of(step)
        shared(k).wait_recv()
        rotated_ref[k] = (weight[0] * panels[0, k, 0] + weight[1] * panels[1, k, 0]
                          + weight[2] * panels[0, k, 1] + weight[3] * panels[1, k, 1])
    for step in [0] + near:
        k = chunk_of(step)
        to_mate(k).wait_send()
        if step != 0:
            scatter(k).wait_send()
            gather(k).wait_send()
        share(k).wait_send()
    for which in range(2):
        to_across(which).wait_send()


def filter_kernel(width, orb_hbm, pot_hbm, degree_ref, owner_ref, rot_ref, ymat_hbm, pmat_hbm,
                  result_ref, out_ref, field, inner, diag, send_sem, recv_sem, pot_send, pot_recv,
                  hand_send, hand_recv, go_sem, vouch_sem, load_sem, orb_ref, pot_ref, ymat_ref,
                  pmat_ref, *rotation_scratch):
    count = lax.axis_size("dom")
    me = lax.axis_index("dom")
    has_left = me > 0
    has_right = me < count - 1
    half = RADIUS
    w = width

    def to_left(src, dst, ssem, rsem):
        return pltpu.make_async_remote_copy(
            src_ref=src, dst_ref=dst, send_sem=ssem, recv_sem=rsem,
            device_id={"dom": jnp.maximum(me - 1, 0)}, device_id_type=MESH)

    def to_right(src, dst, ssem, rsem):
        return pltpu.make_async_remote_copy(
            src_ref=src, dst_ref=dst, send_sem=ssem, recv_sem=rsem,
            device_id={"dom": jnp.minimum(me + 1, count - 1)}, device_id_type=MESH)

    def copies(r):
        src = field.at[r, pl.ds(w, w)]
        left = to_left(src, field.at[r, pl.ds(2 * w, w)], send_sem.at[r, 0], recv_sem.at[r, 0])
        right = to_right(src, field.at[r, pl.ds(0, w)], send_sem.at[r, 1], recv_sem.at[r, 1])
        return left, right

    z, pair, core = seat()
    mate = at(z, pair, 1 - core)
    is_first = core == 0
    is_second = core == 1
    low_half, high_half = pl.ds(0, half), pl.ds(half + w, half)
    pot_left = lambda: to_left(pot_ref.at[pl.ds(0, half)], diag.at[high_half], pot_send.at[0], pot_recv.at[0])
    pot_right = lambda: to_right(pot_ref.at[pl.ds(w - half, half)], diag.at[low_half], pot_send.at[1], pot_recv.at[1])

    def hand(side):
        part = diag.at[high_half if side else low_half]
        return pltpu.make_async_remote_copy(
            src_ref=part, dst_ref=part, send_sem=hand_send.at[side], recv_sem=hand_recv.at[side],
            device_id=mate, device_id_type=MESH)

    def on(condition, *actions):
        @pl.when(condition)
        def _():
            for action in actions:
                action()

    peers = [{"dom": lax.rem(me + shift, count)} for shift in (1, count - 1)] + rotation_peers()
    barrier = pltpu.get_barrier_semaphore()
    for peer in peers:
        pl.semaphore_signal(barrier, inc=1, device_id=peer, device_id_type=MESH)
    loads = [
        pltpu.make_async_copy(src, dst, load_sem.at[slot])
        for slot, (src, dst) in enumerate((
            (orb_hbm, orb_ref), (pot_hbm, pot_ref), (ymat_hbm, ymat_ref), (pmat_hbm, pmat_ref)))]
    for load in loads:
        load.start()
    loads[0].wait()
    field[0, w:2 * w] = orb_ref[...].astype(jnp.float32)
    loads[1].wait()
    pl.semaphore_wait(barrier, len(peers))

    def start(r):
        on(has_left, lambda: copies(r)[0].start())
        on(has_right, lambda: copies(r)[1].start())

    def sent(r):
        on(has_left, lambda: copies(r)[0].wait_send())
        on(has_right, lambda: copies(r)[1].wait_send())

    def arrive(r):
        on(has_left, lambda: copies(r)[1].wait_recv())
        on(has_right, lambda: copies(r)[0].wait_recv())

    @pl.when(is_first)
    def _():
        start(0)
        sent(0)
        pl.semaphore_signal(go_sem, inc=1, device_id=mate, device_id_type=MESH)

    @pl.when(is_second)
    def _():
        on(has_left, lambda: pot_left().start())
        on(has_right, lambda: pot_right().start())
        pl.semaphore_wait(go_sem, 1)
        start(0)

    @pl.when(jnp.logical_not(has_left))
    def _():
        for r in range(ROUNDS):
            field[r, 0:w] = jnp.zeros((w,) + field.shape[2:], jnp.float32)
        diag[0:half] = jnp.zeros((half,) + diag.shape[1:], jnp.float32)

    @pl.when(jnp.logical_not(has_right))
    def _():
        for r in range(ROUNDS):
            field[r, 2 * w:3 * w] = jnp.zeros((w,) + field.shape[2:], jnp.float32)
        diag[half + w:2 * half + w] = jnp.zeros((half,) + diag.shape[1:], jnp.float32)

    diag[half:half + w] = pot_ref[...]
    loads[2].wait()
    loads[3].wait()

    @pl.when(is_second)
    def _():
        on(has_left, lambda: pot_right().wait_recv(), lambda: hand(0).start())
        on(has_right, lambda: pot_left().wait_recv(), lambda: hand(1).start())

    @pl.when(is_first)
    def _():
        on(has_left, lambda: hand(0).wait_recv())
        on(has_right, lambda: hand(1).wait_recv())

    planes, cells = field.shape[2], field.shape[3]
    rows = half * planes
    left_mask = jnp.where(has_left, 1.0, 0.0).astype(jnp.float32)
    right_mask = jnp.where(has_right, 1.0, 0.0).astype(jnp.float32)
    degree = degree_ref[0]

    def along_yp(centre):
        flat = centre.reshape(2 * rows, cells)
        high = flat.astype(jnp.bfloat16)
        rest = (flat - high.astype(jnp.float32)).astype(jnp.bfloat16)
        both = jnp.dot(jnp.concatenate([high, rest], axis=1), ymat_ref[...], preferred_element_type=jnp.float32)
        total = both[:, :cells] + both[:, cells:]
        stacked = jnp.concatenate([
            jnp.concatenate([high[:rows], high[rows:]], axis=1),
            jnp.concatenate([rest[:rows], rest[rows:]], axis=1)], axis=0)
        both = jnp.dot(pmat_ref[...], stacked, preferred_element_type=jnp.float32)
        both = both[:rows] + both[rows:]
        both = jnp.concatenate([both[:, :cells], both[:, cells:]], axis=0)
        return (total + both).reshape(centre.shape)

    def along_x(ref, low, diag_low, layers):
        total = (diag[diag_low:diag_low + layers] * SCALE + CENTRE) * ref[low:low + layers]
        for offset in range(1, RADIUS + 1):
            total = total + SIDE[offset] * (
                ref[low + offset:low + offset + layers] + ref[low - offset:low - offset + layers])
        return total

    for r in range(ROUNDS):
        now = field.at[r]
        own_part = along_yp(now[w:2 * w])
        arrive(r)
        halo_part = along_yp(jnp.concatenate([now[w - half:w], now[2 * w:2 * w + half]], axis=0))
        strips = (
            (0, half, halo_part[:half], left_mask),
            (half, w, own_part, None),
            (half + w, half, halo_part[half:], right_mask),
        )
        for low, layers, part, mask in strips:
            advanced = along_x(now, low + half, low, layers) + part
            advanced = 0.5 * advanced if r == 0 else advanced - inner[low:low + layers]
            inner[low:low + layers] = advanced if mask is None else advanced * mask
        advanced = along_x(inner, half, half, w) + along_yp(inner[half:half + w]) - now[w:2 * w]
        if r + 1 < ROUNDS:
            field[r + 1, w:2 * w] = advanced
            start(r + 1)
        vouch(r + 1, vouch_sem)
        before = out_ref[...] if r > 0 else jnp.zeros_like(advanced)
        before = jnp.where(degree == 2 * r + 1, inner[half:half + w], before)
        out_ref[...] = jnp.where(degree == 2 * r + 2, advanced, before)

    result_ref[0] = out_ref[...].reshape(result_ref.shape[1:])
    rotate(out_ref[...], owner_ref, rot_ref, result_ref.at[1], *rotation_scratch)

    for r in range(1, ROUNDS):
        sent(r)

    @pl.when(is_second)
    def _():
        sent(0)
        on(has_left, lambda: pot_left().wait_send(), lambda: hand(0).wait_send())
        on(has_right, lambda: pot_right().wait_send(), lambda: hand(1).wait_send())


def filter_and_rotate(orbitals, potential, degree, owners, coefficients):
    width, planes, cells = orbitals.shape
    chips = lax.axis_size("orb") // 4
    piece = (width * planes // 8 // chips, 8, cells)
    ymat, pmat = stencil_matrices(planes, cells, RADIUS)
    vmem = pl.BlockSpec(memory_space=pltpu.VMEM)
    smem = pl.BlockSpec(memory_space=pltpu.SMEM)
    hbm = pl.BlockSpec(memory_space=pl.ANY)
    buffer = lambda *lead: pltpu.VMEM(lead + piece, jnp.float32)
    result = pl.pallas_call(
        lambda *refs: filter_kernel(width, *refs),
        out_shape=pltpu.VMEM((2, chips) + piece, jnp.float32),
        in_specs=[hbm, hbm, smem, smem, vmem, hbm, hbm],
        out_specs=vmem,
        scratch_shapes=[
            pltpu.VMEM(orbitals.shape, jnp.float32),
            pltpu.VMEM((ROUNDS, 3 * width, planes, cells), jnp.float32),
            pltpu.VMEM((2 * width, planes, cells), jnp.float32),
            pltpu.VMEM((width + 2 * RADIUS, planes, cells), jnp.float32),
            pltpu.SemaphoreType.DMA((ROUNDS, 2)),
            pltpu.SemaphoreType.DMA((ROUNDS, 2)),
            pltpu.SemaphoreType.DMA((2,)),
            pltpu.SemaphoreType.DMA((2,)),
            pltpu.SemaphoreType.DMA((2,)),
            pltpu.SemaphoreType.DMA((2,)),
            pltpu.SemaphoreType.REGULAR,
            pltpu.SemaphoreType.REGULAR((2, ROUNDS)),
            pltpu.SemaphoreType.DMA((4,)),
            pltpu.VMEM(orbitals.shape, orbitals.dtype),
            pltpu.VMEM(potential.shape, jnp.float32),
            pltpu.VMEM(ymat.shape, jnp.bfloat16),
            pltpu.VMEM(pmat.shape, jnp.bfloat16),
            buffer(chips), buffer(chips, 2), buffer(chips, 2), buffer(chips, 2), buffer(chips, 2),
            buffer(2), buffer(2), buffer(2, chips, 2),
            pltpu.SemaphoreType.DMA((5, 2, chips)),
        ],
        compiler_params=pltpu.CompilerParams(collective_id=0, has_side_effects=True),
        name="filter_rotate",
    )(orbitals, potential, degree, owners, coefficients, jnp.asarray(ymat), jnp.asarray(pmat))
    result = result.reshape((2,) + orbitals.shape)
    return result[0], result[1]


def per_device(orbitals, potential, degree, owners, rotation):
    layers = jnp.transpose(orbitals[0], (1, 0, 2))
    filtered, rotated = filter_and_rotate(
        layers, jnp.transpose(potential, (1, 0, 2)), degree, owners,
        rotation.reshape(1, STEPS))
    return jnp.transpose(filtered, (1, 0, 2))[None], jnp.transpose(rotated, (1, 0, 2))[None]


def solution(mesh):
    placed = (
        P("orb", None, "dom", None),
        P(None, "dom", None),
        P("orb"),
        P(),
        P(None, None, "orb"),
    )
    return jax.shard_map(
        per_device,
        mesh=mesh,
        in_specs=placed,
        out_specs=(P("orb", None, "dom", None), P("orb", None, "dom", None)),
        check_vma=False,
    )
```
